512 devices in a mesh: dp: 16 (over z, core), mp: 8 (over y), expert: 4 (over x).
Axes of the slice: x: 4, y: 8, z: 8, core: 2. Of those that a mesh axis runs over, the one named last changes fastest.
Arguments:
- attn_out: bfloat16 [16384, 2304], P('dp', 'mp'), may hold values from -6 to 6
- residual: float32 [16384, 2304], P(('dp', 'mp', 'expert'))
- proj_weight: bfloat16 [2304, 2304], P('mp'), may hold values from -0.125 to 0.125
- norm_gain: float32 [2304], replicated, may hold values from 0.1 to 1.9
- gate_weight: bfloat16 [8, 2304, 4096], P('mp', None, 'expert'), may hold values from -0.125 to 0.125
- up_weight: bfloat16 [8, 2304, 4096], P('mp', None, 'expert'), may hold values from -0.125 to 0.125
- down_weight: bfloat16 [8, 4096, 2304], P('mp', 'expert'), may hold values from -0.09375 to 0.09375
- routes: int32 [16384, 2], P(('dp', 'mp', 'expert')), may hold values from 0 to 7, as said below
- route_weights: float32 [16384, 2], P(('dp', 'mp', 'expert')), may hold values from 0.2 to 1
Outputs:
- mixed: float32 [16384, 2304], P(('dp', 'mp', 'expert'))
The draws below stay inside these ranges and needn't reach their ends.
Inputs may be any that keep to these rules, and one draw needn't show every extreme that they name: `routes`: the two ids of a row differ. In the rows of each device (aligned blocks of 32 rows, in order) every expert is named by at most 16 rows; one expert, the same in all blocks, is named by exactly 16 rows in every block, and the other 48 names of a block are spread as evenly as possible over the other experts.
All inputs are finite; a program needn't handle non-finite values.
Results may differ from the reference program's by a relative error of at most 0.0015.
Values may be sent and summed in bfloat16 or wider, within the bound.
No kernel may reach another device: no remote copies, remote signals or barrier semaphores. Data moves between devices by JAX's collectives and lax.ppermute only.
A program may use at most 64 MiB of HBM per device.

```python
import math
import jax
import jax.numpy as jnp
from jax import lax

D = 2304
FF = 4096
EXPERTS = 8
ROWS = 32
MOST = 16
UNITS_DEV = 1024
TOKENS = 16384
N_EXPERT = 4


def draw_residual(key, part):
    noise_key, row_key, column_key = jax.random.split(key, 3)
    columns = jnp.arange(D, dtype=jnp.float32) / D
    noise = jax.random.normal(noise_key, (TOKENS, D), jnp.float32)
    row_scale = jnp.exp(jax.random.uniform(row_key, (TOKENS, 1), jnp.float32, 0.0, math.log(10.0)))
    column_scale = jnp.exp(columns * math.log(10.0) + jax.random.uniform(column_key, (1, D), jnp.float32, math.log(0.7), math.log(1.4)))
    return (0.1 * noise * row_scale * column_scale).astype(jnp.float32)


def draw_routes(key, part):
    block_total = TOKENS // ROWS
    hot_key, order_key, row_key = jax.random.split(key, 3)
    hottest = jax.random.randint(hot_key, (), 0, EXPERTS).astype(jnp.int32)
    order_keys = jax.random.split(order_key, block_total)
    row_keys = jax.random.split(row_key, block_total)
    other_count = EXPERTS - 1
    remain = 2 * ROWS - MOST
    even_share = remain // other_count
    leftover = remain % other_count
    counts = jnp.concatenate([jnp.array([MOST], jnp.int32), (even_share + (jnp.arange(other_count) < leftover)).astype(jnp.int32)])
    bounds = jnp.cumsum(counts)
    positions = jnp.arange(2 * ROWS, dtype=jnp.int32)
    segment = jnp.sum((positions[:, None] >= bounds[None, :]).astype(jnp.int32), axis=1)

    def one_block(order_seed, row_seed):
        others = (hottest + 1 + jax.random.permutation(order_seed, other_count).astype(jnp.int32)) % EXPERTS
        ordering = jnp.concatenate([hottest[None], others])
        sequence = ordering[segment]
        shuffle = jax.random.permutation(row_seed, ROWS).astype(jnp.int32)
        return jnp.stack([sequence[shuffle], sequence[shuffle + ROWS]], axis=1)
    return jax.vmap(one_block)(order_keys, row_keys).reshape(TOKENS, 2).astype(jnp.int32)


def shard_levels(key, shape, pieces, low, largest):
    def one(axis_at, parts):
        steps = jax.random.uniform(jax.random.fold_in(jax.random.fold_in(key, 6), axis_at), (parts,), jnp.float32, low / len(pieces), largest / len(pieces))
        return jnp.repeat(jnp.exp(steps), shape[axis_at] // parts).reshape((-1,) + (1,) * (len(shape) - axis_at - 1))

    factor_of = one(*pieces[0])
    for cut in pieces[1:]:
        factor_of = factor_of * one(*cut)
    return factor_of


def normal_values(own_key, dims, scale, most, pieces=(), kind=jnp.bfloat16):
    loudness = shard_levels(own_key, dims, pieces, -0.22, 0.18) if pieces else 1.0
    result = jax.random.normal(own_key, dims, jnp.float32) * scale * loudness
    return jnp.minimum(jnp.maximum(result, -most), most).astype(kind)


def setup_inputs(seed: int = 0) -> dict:
    key_list = jax.random.split(jax.random.key(seed), 10)
    return {
        "attn_out": normal_values(key_list[0], (TOKENS, D), 1.0, 6.0, ((0, 16), (1, 8))),
        "residual": draw_residual(jax.random.fold_in(key_list[9], 71), 0),
        "proj_weight": normal_values(key_list[2], (D, D), D ** -0.5, 0.125, ((0, 8),)),
        "norm_gain": jnp.clip(1.0 + 0.18 * jax.random.normal(key_list[3], (D,), jnp.float32), 0.1, 1.9),
        "gate_weight": normal_values(key_list[4], (EXPERTS, D, FF), D ** -0.5, 0.125, ((0, 8), (2, 4))),
        "up_weight": normal_values(key_list[5], (EXPERTS, D, FF), D ** -0.5, 0.125, ((0, 8), (2, 4))),
        "down_weight": normal_values(key_list[6], (EXPERTS, FF, D), FF ** -0.5, 0.09375, ((0, 8), (1, 4))),
        "routes": draw_routes(jax.random.fold_in(key_list[9], 71), 0),
        "route_weights": jnp.clip(0.2 + 0.8 * jax.random.uniform(key_list[8], (TOKENS, 2), jnp.float32) ** shard_levels(key_list[8], (TOKENS, 2), ((0, 512),), -0.2, 0.2), 0.2, 1.0),
    }


EPSILON = 1e-06

def reference(attn_out, residual, proj_weight, norm_gain, gate_weight, up_weight, down_weight, routes, route_weights):
    projected = jnp.dot(attn_out, proj_weight, preferred_element_type=jnp.float32)
    hidden_state = residual + projected
    inverse_rms = lax.rsqrt(lax.optimization_barrier(jnp.mean(hidden_state * hidden_state, axis=1, keepdims=True)) + EPSILON)
    normed = (hidden_state * inverse_rms * norm_gain).astype(jnp.bfloat16)
    capacity = MOST * (TOKENS // ROWS)
    expert_ids = routes.reshape(-1)
    collected = jnp.zeros((TOKENS * 2, D), jnp.float32)
    for expert in range(EXPERTS):
        chosen = expert_ids == expert
        indices = jnp.nonzero(chosen, size=capacity, fill_value=0)[0].astype(jnp.int32)
        in_range = jnp.arange(capacity, dtype=jnp.int32) < jnp.sum(chosen.astype(jnp.int32))
        selected = normed[indices // 2]
        gate_part = jnp.dot(selected, gate_weight[expert], preferred_element_type=jnp.float32)
        up_part = jnp.dot(selected, up_weight[expert], preferred_element_type=jnp.float32)
        activation = (jax.nn.silu(gate_part) * up_part).astype(jnp.bfloat16)
        accumulated = jnp.zeros((capacity, D), jnp.float32)
        for block_index in range(N_EXPERT):
            lower = block_index * UNITS_DEV
            block_sum = jnp.dot(activation[:, lower:lower + UNITS_DEV], down_weight[expert, lower:lower + UNITS_DEV], preferred_element_type=jnp.float32)
            accumulated = accumulated + lax.optimization_barrier(block_sum.astype(jnp.bfloat16)).astype(jnp.float32)
        expert_out = accumulated.astype(jnp.bfloat16).astype(jnp.float32)
        collected = collected.at[indices].add(jnp.where(in_range[:, None], expert_out, jnp.float32(0.0)))
    collected = collected.reshape(TOKENS, 2, D)
    return hidden_state + route_weights[:, 0:1] * collected[:, 0] + route_weights[:, 1:2] * collected[:, 1]
```

```python
import jax
import jax.numpy as jnp
from jax import lax
from jax.experimental import pallas as pl
from jax.experimental.pallas import tpu as pltpu
from jax.sharding import PartitionSpec as P

EXPERTS = 8
MOST = 16
EPSILON = 1e-06

UP_CHUNK = 256
DOWN_CHUNK = 768


def ffn_kernel(x_ref, gate_ref, up_ref, down_ref, out_ref, act_ref):
    step = pl.program_id(0)
    up_steps = act_ref.shape[0]

    @pl.when(step < up_steps)
    def _():
        rows = x_ref[...]
        gate = jnp.dot(rows, gate_ref[...], preferred_element_type=jnp.float32)
        up = jnp.dot(rows, up_ref[...], preferred_element_type=jnp.float32)
        act_ref[step] = (gate / (1.0 + jnp.exp(-gate)) * up).astype(jnp.bfloat16)

    @pl.when(step >= up_steps)
    def _():
        total = jnp.dot(act_ref[0], down_ref[0], preferred_element_type=jnp.float32)
        for part in range(1, up_steps):
            total += jnp.dot(act_ref[part], down_ref[part], preferred_element_type=jnp.float32)
        out_ref[...] = total.astype(jnp.bfloat16)


def ffn(rows, gate_weight, up_weight, down_weight):
    count, features = rows.shape
    units = gate_weight.shape[1]
    up_steps = units // UP_CHUNK
    down_steps = features // DOWN_CHUNK
    return pl.pallas_call(
        ffn_kernel,
        out_shape=jax.ShapeDtypeStruct((count, features), jnp.bfloat16),
        grid=(up_steps + down_steps,),
        in_specs=[
            pl.BlockSpec((count, features), lambda i: (0, 0)),
            pl.BlockSpec((features, UP_CHUNK), lambda i: (0, jnp.minimum(i, up_steps - 1))),
            pl.BlockSpec((features, UP_CHUNK), lambda i: (0, jnp.minimum(i, up_steps - 1))),
            pl.BlockSpec(
                (up_steps, UP_CHUNK, DOWN_CHUNK), lambda i: (0, 0, jnp.maximum(i - up_steps, 0))
            ),
        ],
        out_specs=pl.BlockSpec((count, DOWN_CHUNK), lambda i: (0, jnp.maximum(i - up_steps, 0))),
        scratch_shapes=[pltpu.VMEM((up_steps, count, UP_CHUNK), jnp.bfloat16)],
        compiler_params=pltpu.CompilerParams(vmem_limit_bytes=40 << 20),
    )(rows, gate_weight, up_weight, down_weight.reshape(up_steps, UP_CHUNK, features))


def body(
    attn_out,
    residual,
    proj_weight,
    norm_gain,
    gate_weight,
    up_weight,
    down_weight,
    routes,
    route_weights,
):
    model_parts = lax.axis_size("mp")
    unit_parts = lax.axis_size("expert")
    row_count = residual.shape[0]
    features = residual.shape[1]
    blocks = attn_out.reshape(model_parts, unit_parts, row_count, attn_out.shape[1])
    picked = lax.dynamic_index_in_dim(blocks, lax.axis_index("expert"), axis=1, keepdims=False)
    picked = picked.reshape(model_parts * row_count, attn_out.shape[1])
    parts = jnp.dot(picked, proj_weight, preferred_element_type=jnp.float32).astype(jnp.bfloat16)
    parts = parts.reshape(model_parts, row_count, features)
    parts = lax.all_to_all(parts, "mp", split_axis=0, concat_axis=0, tiled=True)
    hidden_state = residual + jnp.sum(parts, axis=0, dtype=jnp.float32)
    inverse_rms = lax.rsqrt(jnp.mean(hidden_state * hidden_state, axis=1, keepdims=True) + EPSILON)
    normed = (hidden_state * inverse_rms * norm_gain).astype(jnp.bfloat16)
    expert_ids = routes.reshape(-1)
    onehot = (expert_ids[:, None] == jnp.arange(EXPERTS, dtype=jnp.int32)[None, :]).astype(
        jnp.int32
    )
    before = jnp.cumsum(onehot, axis=0) - onehot
    position = jnp.sum(before * onehot, axis=1)
    target = (expert_ids * MOST + position).reshape(row_count, 2)
    slots = jnp.arange(EXPERTS * MOST, dtype=jnp.int32)
    first = target[:, 0][:, None] == slots[None, :]
    second = target[:, 1][:, None] == slots[None, :]
    placement = (first | second).astype(jnp.bfloat16)
    outgoing = lax.dot_general(
        placement, normed, (((0,), (0,)), ((), ())), preferred_element_type=jnp.float32
    ).astype(jnp.bfloat16)
    outgoing = outgoing.reshape(model_parts, MOST, features)
    arrived = lax.all_to_all(outgoing, "mp", split_axis=0, concat_axis=0, tiled=True)
    copies = jnp.broadcast_to(arrived[None], (unit_parts, model_parts, MOST, features))
    copies = lax.all_to_all(copies, "expert", split_axis=0, concat_axis=0, tiled=True)
    rows = copies.reshape(unit_parts * model_parts * MOST, features)
    partial_value = ffn(rows, gate_weight[0], up_weight[0], down_weight[0])
    partial_value = partial_value.reshape(unit_parts, model_parts, MOST, features)
    returned = lax.all_to_all(partial_value, "expert", split_axis=0, concat_axis=0, tiled=True)
    outputs = jnp.sum(returned, axis=0, dtype=jnp.float32).astype(jnp.bfloat16)
    outputs = lax.all_to_all(outputs, "mp", split_axis=0, concat_axis=0, tiled=True)
    expert_out = outputs.reshape(EXPERTS * MOST, features)
    one = jnp.dot(first.astype(jnp.bfloat16), expert_out, preferred_element_type=jnp.float32)
    two = jnp.dot(second.astype(jnp.bfloat16), expert_out, preferred_element_type=jnp.float32)
    return hidden_state + route_weights[:, 0:1] * one + route_weights[:, 1:2] * two


def solution(mesh):
    in_specs = (
        P("dp", "mp"),
        P(("dp", "mp", "expert"), None),
        P("mp", None),
        P(),
        P("mp", None, "expert"),
        P("mp", None, "expert"),
        P("mp", "expert", None),
        P(("dp", "mp", "expert"), None),
        P(("dp", "mp", "expert"), None),
    )
    out_specs = P(("dp", "mp", "expert"), None)
    return jax.shard_map(body, mesh=mesh, in_specs=in_specs, out_specs=out_specs, check_vma=False)
```

```python
import jax
import jax.numpy as jnp
from jax import lax
from jax.experimental import pallas as pl
from jax.experimental.pallas import tpu as pltpu
from jax.sharding import PartitionSpec as P

EXPERTS = 8
MOST = 16
PIECES = 2
EPSILON = 1e-06

UP_CHUNK = 256
DOWN_CHUNK = 768


def ffn_kernel(x_ref, gate_ref, up_ref, down_ref, out_ref, act_ref):
    step = pl.program_id(0)
    up_steps = act_ref.shape[0]

    @pl.when(step < up_steps)
    def _():
        rows = x_ref[...]
        gate = jnp.dot(rows, gate_ref[...], preferred_element_type=jnp.float32)
        up = jnp.dot(rows, up_ref[...], preferred_element_type=jnp.float32)
        act_ref[step] = (gate / (1.0 + jnp.exp(-gate)) * up).astype(jnp.bfloat16)

    @pl.when(step >= up_steps)
    def _():
        total = jnp.dot(act_ref[0], down_ref[0], preferred_element_type=jnp.float32)
        for part in range(1, up_steps):
            total += jnp.dot(act_ref[part], down_ref[part], preferred_element_type=jnp.float32)
        out_ref[...] = total.astype(jnp.bfloat16)


def ffn(rows, gate_weight, up_weight, down_weight):
    count, features = rows.shape
    units = gate_weight.shape[1]
    up_steps = units // UP_CHUNK
    down_steps = features // DOWN_CHUNK
    return pl.pallas_call(
        ffn_kernel,
        out_shape=jax.ShapeDtypeStruct((count, features), jnp.bfloat16),
        grid=(up_steps + down_steps,),
        in_specs=[
            pl.BlockSpec((count, features), lambda i: (0, 0)),
            pl.BlockSpec((features, UP_CHUNK), lambda i: (0, jnp.minimum(i, up_steps - 1))),
            pl.BlockSpec((features, UP_CHUNK), lambda i: (0, jnp.minimum(i, up_steps - 1))),
            pl.BlockSpec(
                (up_steps, UP_CHUNK, DOWN_CHUNK), lambda i: (0, 0, jnp.maximum(i - up_steps, 0))
            ),
        ],
        out_specs=pl.BlockSpec((count, DOWN_CHUNK), lambda i: (0, jnp.maximum(i - up_steps, 0))),
        scratch_shapes=[pltpu.VMEM((up_steps, count, UP_CHUNK), jnp.bfloat16)],
        compiler_params=pltpu.CompilerParams(vmem_limit_bytes=40 << 20),
    )(
        rows,
        pltpu.with_memory_space_constraint(gate_weight, pltpu.HBM),
        pltpu.with_memory_space_constraint(up_weight, pltpu.HBM),
        pltpu.with_memory_space_constraint(
            down_weight.reshape(up_steps, UP_CHUNK, features), pltpu.HBM
        ),
    )


def body(
    attn_out,
    residual,
    proj_weight,
    norm_gain,
    gate_weight,
    up_weight,
    down_weight,
    routes,
    route_weights,
):
    model_parts = lax.axis_size("mp")
    unit_parts = lax.axis_size("expert")
    row_count = residual.shape[0]
    features = residual.shape[1]
    blocks = attn_out.reshape(model_parts, unit_parts, row_count, attn_out.shape[1])
    picked = lax.dynamic_index_in_dim(blocks, lax.axis_index("expert"), axis=1, keepdims=False)
    picked = picked.reshape(model_parts * row_count, attn_out.shape[1])
    parts = jnp.dot(picked, proj_weight, preferred_element_type=jnp.float32).astype(jnp.float16)
    parts = parts.reshape(model_parts, row_count, features)
    parts = lax.all_to_all(parts, "mp", split_axis=0, concat_axis=0, tiled=True)
    hidden_state = residual + jnp.sum(parts, axis=0, dtype=jnp.float32)
    inverse_rms = lax.rsqrt(jnp.mean(hidden_state * hidden_state, axis=1, keepdims=True) + EPSILON)
    normed = (hidden_state * inverse_rms * norm_gain).astype(jnp.bfloat16)
    expert_ids = routes.reshape(-1)
    onehot = (expert_ids[:, None] == jnp.arange(EXPERTS, dtype=jnp.int32)[None, :]).astype(
        jnp.int32
    )
    before = jnp.cumsum(onehot, axis=0) - onehot
    position = jnp.sum(before * onehot, axis=1)
    target = (expert_ids * MOST + position).reshape(row_count, 2)
    slots = jnp.arange(EXPERTS * MOST, dtype=jnp.int32)
    first = target[:, 0][:, None] == slots[None, :]
    second = target[:, 1][:, None] == slots[None, :]
    placement = (first | second).astype(jnp.bfloat16)
    outgoing = lax.dot_general(
        placement, normed, (((0,), (0,)), ((), ())), preferred_element_type=jnp.float32
    ).astype(jnp.bfloat16)
    outgoing = outgoing.reshape(model_parts, MOST, features)
    arrived = lax.all_to_all(outgoing, "mp", split_axis=0, concat_axis=0, tiled=True)
    depth = MOST // PIECES
    sums = []
    for piece in range(PIECES):
        part = arrived[:, piece * depth : (piece + 1) * depth]
        copies = jnp.broadcast_to(part[None], (unit_parts,) + part.shape)
        copies = lax.all_to_all(copies, "expert", split_axis=0, concat_axis=0, tiled=True)
        rows = copies.reshape(-1, features)
        partial_value = ffn(rows, gate_weight[0], up_weight[0], down_weight[0])
        partial_value = partial_value.reshape(copies.shape)
        returned = lax.all_to_all(partial_value, "expert", split_axis=0, concat_axis=0, tiled=True)
        sums.append(jnp.sum(returned, axis=0, dtype=jnp.float32).astype(jnp.bfloat16))
    outputs = jnp.concatenate(sums, axis=1)
    outputs = lax.all_to_all(outputs, "mp", split_axis=0, concat_axis=0, tiled=True)
    expert_out = outputs.reshape(EXPERTS * MOST, features)
    one = jnp.dot(first.astype(jnp.bfloat16), expert_out, preferred_element_type=jnp.float32)
    two = jnp.dot(second.astype(jnp.bfloat16), expert_out, preferred_element_type=jnp.float32)
    return hidden_state + route_weights[:, 0:1] * one + route_weights[:, 1:2] * two


def solution(mesh):
    in_specs = (
        P("dp", "mp"),
        P(("dp", "mp", "expert"), None),
        P("mp", None),
        P(),
        P("mp", None, "expert"),
        P("mp", None, "expert"),
        P("mp", "expert", None),
        P(("dp", "mp", "expert"), None),
        P(("dp", "mp", "expert"), None),
    )
    out_specs = P(("dp", "mp", "expert"), None)
    return jax.shard_map(body, mesh=mesh, in_specs=in_specs, out_specs=out_specs, check_vma=False)
```

```python
import functools

import jax
import jax.numpy as jnp
from jax import lax
from jax.experimental import pallas as pl
from jax.experimental.pallas import tpu as pltpu
from jax.sharding import PartitionSpec as P

EXPERTS = 8
MOST = 16
EPSILON = 1e-06

UNIT_CHUNK = 512
OUT_CHUNK = 1152


def ffn_kernel(count, *refs):
    row_refs, refs = refs[:count], refs[count:]
    (gate_hbm, up_hbm, down_hbm), refs = refs[:3], refs[3:]
    out_refs, refs = refs[:count], refs[count:]
    rows_ref, act_ref, gate_ref, up_ref, down_ref, gate_sem, up_sem, down_sem = refs
    depth = row_refs[0].shape[0]
    unit_steps = gate_sem.shape[0]
    out_steps = down_sem.shape[0]

    def columns(step, width):
        return pl.ds(step * width, width)

    gate_copies, up_copies, down_copies = [], [], []
    for step in range(unit_steps):
        at = columns(step, UNIT_CHUNK)
        gate_copies.append(
            pltpu.make_async_copy(gate_hbm.at[:, at], gate_ref.at[:, at], gate_sem.at[step])
        )
        up_copies.append(pltpu.make_async_copy(up_hbm.at[:, at], up_ref.at[:, at], up_sem.at[step]))
    for step in range(out_steps):
        at = columns(step, OUT_CHUNK)
        down_copies.append(
            pltpu.make_async_copy(down_hbm.at[:, at], down_ref.at[:, at], down_sem.at[step])
        )
    for step in range(unit_steps):
        gate_copies[step].start()
        up_copies[step].start()
    for step in range(out_steps):
        down_copies[step].start()
    for piece in range(count):
        rows_ref[pl.ds(piece * depth, depth), :] = row_refs[piece][...]
    for step in range(unit_steps):
        at = columns(step, UNIT_CHUNK)
        gate_copies[step].wait()
        up_copies[step].wait()
        gate = jnp.dot(rows_ref[...], gate_ref[:, at], preferred_element_type=jnp.float32)
        up = jnp.dot(rows_ref[...], up_ref[:, at], preferred_element_type=jnp.float32)
        act_ref[:, at] = (gate / (1.0 + jnp.exp(-gate)) * up).astype(jnp.bfloat16)
    for step in range(out_steps):
        at = columns(step, OUT_CHUNK)
        down_copies[step].wait()
        out = jnp.dot(act_ref[...], down_ref[:, at], preferred_element_type=jnp.float32)
        for piece in range(count):
            out_refs[piece][:, at] = out[piece * depth : (piece + 1) * depth].astype(jnp.bfloat16)


def ffn(pieces, *weights):
    count = len(pieces)
    depth, features = pieces[0].shape
    units = weights[0].shape[1]
    vmem = pl.BlockSpec(memory_space=pltpu.VMEM)
    hbm = pl.BlockSpec(memory_space=pltpu.HBM)
    return pl.pallas_call(
        functools.partial(ffn_kernel, count),
        out_shape=[jax.ShapeDtypeStruct((depth, features), jnp.bfloat16)] * count,
        in_specs=[vmem] * count + [hbm] * 3,
        out_specs=[vmem] * count,
        scratch_shapes=[
            pltpu.VMEM((count * depth, features), jnp.bfloat16),
            pltpu.VMEM((count * depth, units), jnp.bfloat16),
            pltpu.VMEM((features, units), jnp.bfloat16),
            pltpu.VMEM((features, units), jnp.bfloat16),
            pltpu.VMEM((units, features), jnp.bfloat16),
            pltpu.SemaphoreType.DMA((units // UNIT_CHUNK,)),
            pltpu.SemaphoreType.DMA((units // UNIT_CHUNK,)),
            pltpu.SemaphoreType.DMA((features // OUT_CHUNK,)),
        ],
        compiler_params=pltpu.CompilerParams(vmem_limit_bytes=40 << 20),
        cost_estimate=pl.CostEstimate(
            flops=6 * count * depth * features * units,
            transcendentals=count * depth * units,
            bytes_accessed=6 * features * units + 4 * count * depth * features,
        ),
    )(*pieces, *(pltpu.with_memory_space_constraint(w, pltpu.HBM) for w in weights))


def body(
    attn_out,
    residual,
    proj_weight,
    norm_gain,
    gate_weight,
    up_weight,
    down_weight,
    routes,
    route_weights,
):
    model_parts = lax.axis_size("mp")
    unit_parts = lax.axis_size("expert")
    row_count = residual.shape[0]
    features = residual.shape[1]
    blocks = attn_out.reshape(model_parts, unit_parts, row_count, attn_out.shape[1])
    picked = lax.dynamic_index_in_dim(blocks, lax.axis_index("expert"), axis=1, keepdims=False)
    picked = picked.reshape(model_parts * row_count, attn_out.shape[1])
    parts = jnp.dot(picked, proj_weight, preferred_element_type=jnp.float32).astype(jnp.float16)
    parts = parts.reshape(model_parts, row_count, features)
    parts = lax.all_to_all(parts, "mp", split_axis=0, concat_axis=0, tiled=True)
    hidden_state = residual + jnp.sum(parts, axis=0, dtype=jnp.float32)
    inverse_rms = lax.rsqrt(jnp.mean(hidden_state * hidden_state, axis=1, keepdims=True) + EPSILON)
    normed = (hidden_state * inverse_rms * norm_gain).astype(jnp.bfloat16)
    expert_ids = routes.reshape(-1)
    onehot = (expert_ids[:, None] == jnp.arange(EXPERTS, dtype=jnp.int32)[None, :]).astype(
        jnp.int32
    )
    before = jnp.cumsum(onehot, axis=0) - onehot
    position = jnp.sum(before * onehot, axis=1)
    target = (expert_ids * MOST + position).reshape(row_count, 2)
    slots = jnp.arange(EXPERTS * MOST, dtype=jnp.int32)
    first = target[:, 0][:, None] == slots[None, :]
    second = target[:, 1][:, None] == slots[None, :]
    placement = (first | second).astype(jnp.bfloat16)
    outgoing = lax.dot_general(
        placement, normed, (((0,), (0,)), ((), ())), preferred_element_type=jnp.float32
    ).astype(jnp.bfloat16)
    outgoing = outgoing.reshape(model_parts, MOST, features)
    arrived = lax.all_to_all(outgoing, "mp", split_axis=0, concat_axis=0, tiled=True)
    own = arrived.reshape(model_parts * MOST, features)
    weights = (gate_weight[0], up_weight[0], down_weight[0])

    def shift(value, by):
        return lax.ppermute(
            value, "expert", [(i, (i + by) % unit_parts) for i in range(unit_parts)]
        )

    before_rows = shift(own, 1)
    after_rows = shift(own, -1)
    (own_sum,) = ffn([own], *weights)
    far_rows = shift(lax.optimization_barrier((own, own_sum))[0], 2)
    before_sum, after_sum = ffn([before_rows, after_rows], *weights)
    back_after = shift(before_sum, -1)
    back_before = shift(after_sum, 1)
    far_rows = lax.optimization_barrier((far_rows, before_sum))[0]
    (far_sum,) = ffn([far_rows], *weights)
    back_far = shift(far_sum, 2)
    outputs = own_sum.astype(jnp.float32)
    for value in (back_after, back_before, back_far):
        outputs += value.astype(jnp.float32)
    outputs = outputs.astype(jnp.bfloat16).reshape(model_parts, MOST, features)
    outputs = lax.all_to_all(outputs, "mp", split_axis=0, concat_axis=0, tiled=True)
    expert_out = outputs.reshape(EXPERTS * MOST, features)
    one = jnp.dot(first.astype(jnp.bfloat16), expert_out, preferred_element_type=jnp.float32)
    two = jnp.dot(second.astype(jnp.bfloat16), expert_out, preferred_element_type=jnp.float32)
    return hidden_state + route_weights[:, 0:1] * one + route_weights[:, 1:2] * two


def solution(mesh):
    in_specs = (
        P("dp", "mp"),
        P(("dp", "mp", "expert"), None),
        P("mp", None),
        P(),
        P("mp", None, "expert"),
        P("mp", None, "expert"),
        P("mp", "expert", None),
        P(("dp", "mp", "expert"), None),
        P(("dp", "mp", "expert"), None),
    )
    out_specs = P(("dp", "mp", "expert"), None)
    return jax.shard_map(body, mesh=mesh, in_specs=in_specs, out_specs=out_specs, check_vma=False)
```

```python
import functools

import jax
import jax.numpy as jnp
from jax import lax
from jax.experimental import pallas as pl
from jax.experimental.pallas import tpu as pltpu
from jax.sharding import PartitionSpec as P

EXPERTS = 8
MOST = 16
EPSILON = 1e-06

UNIT_CHUNK = 512
OUT_CHUNK = 1152


def ffn_kernel(count, *refs):
    row_refs, refs = refs[:count], refs[count:]
    (gate_hbm, up_hbm, down_hbm), refs = refs[:3], refs[3:]
    out_refs, refs = refs[:count], refs[count:]
    rows_ref, act_ref, gate_ref, up_ref, down_ref, gate_sem, up_sem, down_sem = refs
    depth = row_refs[0].shape[0]
    unit_steps = gate_sem.shape[0]
    out_steps = down_sem.shape[0]

    def columns(step, width):
        return pl.ds(step * width, width)

    gate_copies, up_copies, down_copies = [], [], []
    for step in range(unit_steps):
        at = columns(step, UNIT_CHUNK)
        gate_copies.append(
            pltpu.make_async_copy(gate_hbm.at[:, at], gate_ref.at[:, at], gate_sem.at[step])
        )
        up_copies.append(pltpu.make_async_copy(up_hbm.at[:, at], up_ref.at[:, at], up_sem.at[step]))
    for step in range(out_steps):
        at = columns(step, OUT_CHUNK)
        down_copies.append(
            pltpu.make_async_copy(down_hbm.at[:, at], down_ref.at[:, at], down_sem.at[step])
        )
    for step in range(unit_steps):
        gate_copies[step].start()
        up_copies[step].start()
    for step in range(out_steps):
        down_copies[step].start()
    for piece in range(count):
        rows_ref[pl.ds(piece * depth, depth), :] = row_refs[piece][...]
    for step in range(unit_steps):
        at = columns(step, UNIT_CHUNK)
        gate_copies[step].wait()
        up_copies[step].wait()
        gate = jnp.dot(rows_ref[...], gate_ref[:, at], preferred_element_type=jnp.float32)
        up = jnp.dot(rows_ref[...], up_ref[:, at], preferred_element_type=jnp.float32)
        act_ref[:, at] = (gate / (1.0 + jnp.exp(-gate)) * up).astype(jnp.bfloat16)
    for step in range(out_steps):
        at = columns(step, OUT_CHUNK)
        down_copies[step].wait()
        out = jnp.dot(act_ref[...], down_ref[:, at], preferred_element_type=jnp.float32)
        for piece in range(count):
            out_refs[piece][:, at] = out[piece * depth : (piece + 1) * depth].astype(jnp.bfloat16)


def ffn(pieces, *weights):
    count = len(pieces)
    depth, features = pieces[0].shape
    units = weights[0].shape[1]
    vmem = pl.BlockSpec(memory_space=pltpu.VMEM)
    hbm = pl.BlockSpec(memory_space=pltpu.HBM)
    return pl.pallas_call(
        functools.partial(ffn_kernel, count),
        out_shape=[jax.ShapeDtypeStruct((depth, features), jnp.bfloat16)] * count,
        in_specs=[vmem] * count + [hbm] * 3,
        out_specs=[vmem] * count,
        scratch_shapes=[
            pltpu.VMEM((count * depth, features), jnp.bfloat16),
            pltpu.VMEM((count * depth, units), jnp.bfloat16),
            pltpu.VMEM((features, units), jnp.bfloat16),
            pltpu.VMEM((features, units), jnp.bfloat16),
            pltpu.VMEM((units, features), jnp.bfloat16),
            pltpu.SemaphoreType.DMA((units // UNIT_CHUNK,)),
            pltpu.SemaphoreType.DMA((units // UNIT_CHUNK,)),
            pltpu.SemaphoreType.DMA((features // OUT_CHUNK,)),
        ],
        compiler_params=pltpu.CompilerParams(vmem_limit_bytes=40 << 20),
        cost_estimate=pl.CostEstimate(
            flops=6 * count * depth * features * units,
            transcendentals=count * depth * units,
            bytes_accessed=6 * features * units + 4 * count * depth * features,
        ),
    )(*pieces, *(pltpu.with_memory_space_constraint(w, pltpu.HBM) for w in weights))


def body(
    attn_out,
    residual,
    proj_weight,
    norm_gain,
    gate_weight,
    up_weight,
    down_weight,
    routes,
    route_weights,
):
    model_parts = lax.axis_size("mp")
    unit_parts = lax.axis_size("expert")
    row_count = residual.shape[0]
    features = residual.shape[1]
    picked_rows = jnp.arange(model_parts * row_count, dtype=jnp.int32)
    picked_rows = (
        picked_rows // row_count * unit_parts + lax.axis_index("expert")
    ) * row_count + picked_rows % row_count
    pick = (picked_rows[:, None] == jnp.arange(attn_out.shape[0], dtype=jnp.int32)[None, :]).astype(
        jnp.bfloat16
    )
    picked = jnp.dot(pick, attn_out, preferred_element_type=jnp.float32).astype(jnp.bfloat16)
    parts = jnp.dot(picked, proj_weight, preferred_element_type=jnp.float32).astype(jnp.float16)
    parts = parts.reshape(model_parts, row_count, features)
    parts = lax.all_to_all(parts, "mp", split_axis=0, concat_axis=0, tiled=True)
    hidden_state = residual + jnp.sum(parts, axis=0, dtype=jnp.float32)
    inverse_rms = lax.rsqrt(jnp.mean(hidden_state * hidden_state, axis=1, keepdims=True) + EPSILON)
    normed = (hidden_state * inverse_rms * norm_gain).astype(jnp.bfloat16)
    expert_ids = routes.reshape(-1)
    onehot = (expert_ids[:, None] == jnp.arange(EXPERTS, dtype=jnp.int32)[None, :]).astype(
        jnp.int32
    )
    before = jnp.cumsum(onehot, axis=0) - onehot
    position = jnp.sum(before * onehot, axis=1)
    target = (expert_ids * MOST + position).reshape(row_count, 2)
    slots = jnp.arange(EXPERTS * MOST, dtype=jnp.int32)
    first = target[:, 0][:, None] == slots[None, :]
    second = target[:, 1][:, None] == slots[None, :]
    placement = (first | second).astype(jnp.bfloat16)
    outgoing = lax.dot_general(
        placement, normed, (((0,), (0,)), ((), ())), preferred_element_type=jnp.float32
    ).astype(jnp.bfloat16)
    outgoing = outgoing.reshape(model_parts, MOST, features)
    arrived = lax.all_to_all(outgoing, "mp", split_axis=0, concat_axis=0, tiled=True)
    own = arrived.reshape(model_parts * MOST, features)
    weights = (gate_weight[0], up_weight[0], down_weight[0])

    def shift(value, by):
        return lax.ppermute(
            value, "expert", [(i, (i + by) % unit_parts) for i in range(unit_parts)]
        )

    far_rows = shift(own, 2)
    (own_sum,) = ffn([own], *weights)
    later = lax.optimization_barrier((own, own_sum))[0]
    before_rows = shift(later, 1)
    after_rows = shift(later, -1)
    (far_sum,) = ffn([far_rows], *weights)
    back_far = shift(far_sum, 2)
    before_rows, after_rows, far_sum = lax.optimization_barrier((before_rows, after_rows, far_sum))
    before_sum, after_sum = ffn([before_rows, after_rows], *weights)
    back_after = shift(before_sum, -1)
    after_sum, back_far = lax.optimization_barrier((after_sum, back_far))
    back_before = shift(after_sum, 1)
    outputs = own_sum.astype(jnp.float32)
    for value in (back_after, back_before, back_far):
        outputs += value.astype(jnp.float32)
    outputs = outputs.astype(jnp.bfloat16).reshape(model_parts, MOST, features)
    outputs = lax.all_to_all(outputs, "mp", split_axis=0, concat_axis=0, tiled=True)
    expert_out = outputs.reshape(EXPERTS * MOST, features)
    one = jnp.dot(first.astype(jnp.bfloat16), expert_out, preferred_element_type=jnp.float32)
    two = jnp.dot(second.astype(jnp.bfloat16), expert_out, preferred_element_type=jnp.float32)
    return hidden_state + route_weights[:, 0:1] * one + route_weights[:, 1:2] * two


def solution(mesh):
    in_specs = (
        P("dp", "mp"),
        P(("dp", "mp", "expert"), None),
        P("mp", None),
        P(),
        P("mp", None, "expert"),
        P("mp", None, "expert"),
        P("mp", "expert", None),
        P(("dp", "mp", "expert"), None),
        P(("dp", "mp", "expert"), None),
    )
    out_specs = P(("dp", "mp", "expert"), None)
    return jax.shard_map(body, mesh=mesh, in_specs=in_specs, out_specs=out_specs, check_vma=False)
```

```python
import functools

import jax
import jax.numpy as jnp
from jax import lax
from jax.experimental import pallas as pl
from jax.experimental.pallas import tpu as pltpu
from jax.sharding import PartitionSpec as P

EXPERTS = 8
MOST = 16
EPSILON = 1e-06

UNIT_CHUNK = 512
OUT_CHUNK = 1152


def load_kernel(*refs):
    count = (len(refs) - 1) // 2
    sems = refs[-1]
    copies = [
        pltpu.make_async_copy(refs[i], refs[count + i], sems.at[i]) for i in range(count)
    ]
    for copy in copies:
        copy.start()
    for copy in copies:
        copy.wait()


def load(*weights):
    hbm = pl.BlockSpec(memory_space=pltpu.HBM)
    vmem = pl.BlockSpec(memory_space=pltpu.VMEM)
    total = sum(w.size * w.dtype.itemsize for w in weights)
    return pl.pallas_call(
        load_kernel,
        out_shape=[pltpu.VMEM(w.shape, w.dtype) for w in weights],
        in_specs=[hbm] * len(weights),
        out_specs=[vmem] * len(weights),
        scratch_shapes=[pltpu.SemaphoreType.DMA((len(weights),))],
        compiler_params=pltpu.CompilerParams(vmem_limit_bytes=20 << 20),
        cost_estimate=pl.CostEstimate(flops=0, transcendentals=0, bytes_accessed=2 * total),
    )(*(pltpu.with_memory_space_constraint(w, pltpu.HBM) for w in weights))


def ffn_kernel(count, *refs):
    row_refs, refs = refs[:count], refs[count:]
    (gate_ref, up_ref, down_ref), refs = refs[:3], refs[3:]
    out_refs, refs = refs[:count], refs[count:]
    act_ref = refs[0]
    depth = row_refs[0].shape[0]
    if count == 1:
        rows_ref = row_refs[0]
    else:
        rows_ref = refs[1]
        for piece in range(count):
            rows_ref[pl.ds(piece * depth, depth), :] = row_refs[piece][...]
    for start in range(0, act_ref.shape[1], UNIT_CHUNK):
        at = pl.ds(start, UNIT_CHUNK)
        gate = jnp.dot(rows_ref[...], gate_ref[:, at], preferred_element_type=jnp.float32)
        up = jnp.dot(rows_ref[...], up_ref[:, at], preferred_element_type=jnp.float32)
        act_ref[:, at] = (gate / (1.0 + jnp.exp(-gate)) * up).astype(jnp.bfloat16)
    for start in range(0, down_ref.shape[1], OUT_CHUNK):
        at = pl.ds(start, OUT_CHUNK)
        out = jnp.dot(act_ref[...], down_ref[:, at], preferred_element_type=jnp.float32)
        for piece in range(count):
            out_refs[piece][:, at] = out[piece * depth : (piece + 1) * depth].astype(jnp.bfloat16)


def ffn(pieces, *weights):
    count = len(pieces)
    depth, features = pieces[0].shape
    units = weights[0].shape[1]
    vmem = pl.BlockSpec(memory_space=pltpu.VMEM)
    scratch = [pltpu.VMEM((count * depth, units), jnp.bfloat16)]
    if count > 1:
        scratch.append(pltpu.VMEM((count * depth, features), jnp.bfloat16))
    return pl.pallas_call(
        functools.partial(ffn_kernel, count),
        out_shape=[jax.ShapeDtypeStruct((depth, features), jnp.bfloat16)] * count,
        in_specs=[vmem] * (count + 3),
        out_specs=[vmem] * count,
        scratch_shapes=scratch,
        compiler_params=pltpu.CompilerParams(vmem_limit_bytes=24 << 20),
        cost_estimate=pl.CostEstimate(
            flops=6 * count * depth * features * units,
            transcendentals=count * depth * units,
            bytes_accessed=6 * features * units + 4 * count * depth * features,
        ),
    )(*pieces, *weights)


def body(
    attn_out,
    residual,
    proj_weight,
    norm_gain,
    gate_weight,
    up_weight,
    down_weight,
    routes,
    route_weights,
):
    model_parts = lax.axis_size("mp")
    unit_parts = lax.axis_size("expert")
    row_count = residual.shape[0]
    features = residual.shape[1]
    blocks = attn_out.reshape(model_parts, unit_parts, row_count, attn_out.shape[1])
    picked = lax.dynamic_index_in_dim(blocks, lax.axis_index("expert"), axis=1, keepdims=False)
    picked = picked.reshape(model_parts * row_count, attn_out.shape[1])
    parts = jnp.dot(picked, proj_weight, preferred_element_type=jnp.float32).astype(jnp.float16)
    parts = parts.reshape(model_parts, row_count, features)
    parts = lax.all_to_all(parts, "mp", split_axis=0, concat_axis=0, tiled=True)
    hidden_state = residual + jnp.sum(parts, axis=0, dtype=jnp.float32)
    inverse_rms = lax.rsqrt(jnp.mean(hidden_state * hidden_state, axis=1, keepdims=True) + EPSILON)
    normed = (hidden_state * inverse_rms * norm_gain).astype(jnp.bfloat16)
    expert_ids = routes.reshape(-1)
    onehot = (expert_ids[:, None] == jnp.arange(EXPERTS, dtype=jnp.int32)[None, :]).astype(
        jnp.int32
    )
    before = jnp.cumsum(onehot, axis=0) - onehot
    position = jnp.sum(before * onehot, axis=1)
    target = (expert_ids * MOST + position).reshape(row_count, 2)
    slots = jnp.arange(EXPERTS * MOST, dtype=jnp.int32)
    first = target[:, 0][:, None] == slots[None, :]
    second = target[:, 1][:, None] == slots[None, :]
    placement = (first | second).astype(jnp.bfloat16)
    outgoing = lax.dot_general(
        placement, normed, (((0,), (0,)), ((), ())), preferred_element_type=jnp.float32
    ).astype(jnp.bfloat16)
    outgoing = outgoing.reshape(model_parts, MOST, features)
    arrived = lax.all_to_all(outgoing, "mp", split_axis=0, concat_axis=0, tiled=True)
    own = arrived.reshape(model_parts * MOST, features)

    weights = load(gate_weight[0], up_weight[0], down_weight[0])

    def shift(value, by):
        return lax.ppermute(
            value, "expert", [(i, (i + by) % unit_parts) for i in range(unit_parts)]
        )

    before_rows = shift(own, 1)
    after_rows = shift(own, -1)
    (own_sum,) = ffn([own], *weights)
    far_rows = shift(lax.optimization_barrier((own, own_sum))[0], 2)
    before_sum, after_sum = ffn([before_rows, after_rows], *weights)
    back_after = shift(before_sum, -1)
    back_before = shift(after_sum, 1)
    far_rows = lax.optimization_barrier((far_rows, before_sum))[0]
    (far_sum,) = ffn([far_rows], *weights)
    back_far = shift(far_sum, 2)
    near = own_sum.astype(jnp.float32)
    near = near + back_after.astype(jnp.float32) + back_before.astype(jnp.float32)
    outputs = lax.optimization_barrier(near) + back_far.astype(jnp.float32)
    outputs = outputs.astype(jnp.bfloat16).reshape(model_parts, MOST, features)
    outputs = lax.all_to_all(outputs, "mp", split_axis=0, concat_axis=0, tiled=True)
    expert_out = outputs.reshape(EXPERTS * MOST, features)
    one = jnp.dot(first.astype(jnp.bfloat16), expert_out, preferred_element_type=jnp.float32)
    two = jnp.dot(second.astype(jnp.bfloat16), expert_out, preferred_element_type=jnp.float32)
    return hidden_state + route_weights[:, 0:1] * one + route_weights[:, 1:2] * two


def solution(mesh):
    in_specs = (
        P("dp", "mp"),
        P(("dp", "mp", "expert"), None),
        P("mp", None),
        P(),
        P("mp", None, "expert"),
        P("mp", None, "expert"),
        P("mp", "expert", None),
        P(("dp", "mp", "expert"), None),
        P(("dp", "mp", "expert"), None),
    )
    out_specs = P(("dp", "mp", "expert"), None)
    return jax.shard_map(body, mesh=mesh, in_specs=in_specs, out_specs=out_specs, check_vma=False)
```

```python
import functools

import jax
import jax.numpy as jnp
from jax import lax
from jax.experimental import pallas as pl
from jax.experimental.pallas import tpu as pltpu
from jax.sharding import PartitionSpec as P

EXPERTS = 8
MOST = 16
EPSILON = 1e-06

UNIT_CHUNK = 512
OUT_CHUNK = 1152


def load_kernel(*refs):
    count = (len(refs) - 1) // 2
    sems = refs[-1]
    copies = [
        pltpu.make_async_copy(refs[i], refs[count + i], sems.at[i]) for i in range(count)
    ]
    for copy in copies:
        copy.start()
    for copy in copies:
        copy.wait()


def load(*weights):
    hbm = pl.BlockSpec(memory_space=pltpu.HBM)
    vmem = pl.BlockSpec(memory_space=pltpu.VMEM)
    total = sum(w.size * w.dtype.itemsize for w in weights)
    return pl.pallas_call(
        load_kernel,
        out_shape=[pltpu.VMEM(w.shape, w.dtype) for w in weights],
        in_specs=[hbm] * len(weights),
        out_specs=[vmem] * len(weights),
        scratch_shapes=[pltpu.SemaphoreType.DMA((len(weights),))],
        compiler_params=pltpu.CompilerParams(vmem_limit_bytes=20 << 20),
        cost_estimate=pl.CostEstimate(flops=0, transcendentals=0, bytes_accessed=2 * total),
    )(*(pltpu.with_memory_space_constraint(w, pltpu.HBM) for w in weights))


def ffn_kernel(count, *refs):
    row_refs, refs = refs[:count], refs[count:]
    (gate_ref, up_ref, down_ref), refs = refs[:3], refs[3:]
    out_refs, refs = refs[:count], refs[count:]
    act_ref = refs[0]
    depth = row_refs[0].shape[0]
    if count == 1:
        rows_ref = row_refs[0]
    else:
        rows_ref = refs[1]
        for piece in range(count):
            rows_ref[pl.ds(piece * depth, depth), :] = row_refs[piece][...]
    for start in range(0, act_ref.shape[1], UNIT_CHUNK):
        at = pl.ds(start, UNIT_CHUNK)
        gate = jnp.dot(rows_ref[...], gate_ref[:, at], preferred_element_type=jnp.float32)
        up = jnp.dot(rows_ref[...], up_ref[:, at], preferred_element_type=jnp.float32)
        act_ref[:, at] = (gate / (1.0 + jnp.exp(-gate)) * up).astype(jnp.bfloat16)
    for start in range(0, down_ref.shape[1], OUT_CHUNK):
        at = pl.ds(start, OUT_CHUNK)
        out = jnp.dot(act_ref[...], down_ref[:, at], preferred_element_type=jnp.float32)
        for piece in range(count):
            out_refs[piece][:, at] = out[piece * depth : (piece + 1) * depth].astype(jnp.bfloat16)


def ffn(pieces, *weights):
    count = len(pieces)
    depth, features = pieces[0].shape
    units = weights[0].shape[1]
    vmem = pl.BlockSpec(memory_space=pltpu.VMEM)
    scratch = [pltpu.VMEM((count * depth, units), jnp.bfloat16)]
    if count > 1:
        scratch.append(pltpu.VMEM((count * depth, features), jnp.bfloat16))
    return pl.pallas_call(
        functools.partial(ffn_kernel, count),
        out_shape=[jax.ShapeDtypeStruct((depth, features), jnp.bfloat16)] * count,
        in_specs=[vmem] * (count + 3),
        out_specs=[vmem] * count,
        scratch_shapes=scratch,
        compiler_params=pltpu.CompilerParams(vmem_limit_bytes=24 << 20),
        cost_estimate=pl.CostEstimate(
            flops=6 * count * depth * features * units,
            transcendentals=count * depth * units,
            bytes_accessed=6 * features * units + 4 * count * depth * features,
        ),
    )(*pieces, *weights)


def stream_ffn_kernel(count, *refs):
    row_refs, refs = refs[:count], refs[count:]
    (gate_hbm, up_hbm, down_hbm), refs = refs[:3], refs[3:]
    out_refs, refs = refs[:count], refs[count:]
    rows_ref, act_ref, gate_ref, up_ref, down_ref, gate_sem, up_sem, down_sem = refs
    depth = row_refs[0].shape[0]
    unit_steps = gate_sem.shape[0]
    out_steps = down_sem.shape[0]

    def columns(step, width):
        return pl.ds(step * width, width)

    gate_copies, up_copies, down_copies = [], [], []
    for step in range(unit_steps):
        at = columns(step, UNIT_CHUNK)
        gate_copies.append(
            pltpu.make_async_copy(gate_hbm.at[:, at], gate_ref.at[:, at], gate_sem.at[step])
        )
        up_copies.append(pltpu.make_async_copy(up_hbm.at[:, at], up_ref.at[:, at], up_sem.at[step]))
    for step in range(out_steps):
        at = columns(step, OUT_CHUNK)
        down_copies.append(
            pltpu.make_async_copy(down_hbm.at[:, at], down_ref.at[:, at], down_sem.at[step])
        )
    for step in range(unit_steps):
        gate_copies[step].start()
        up_copies[step].start()
    for step in range(out_steps):
        down_copies[step].start()
    for piece in range(count):
        rows_ref[pl.ds(piece * depth, depth), :] = row_refs[piece][...]
    for step in range(unit_steps):
        at = columns(step, UNIT_CHUNK)
        gate_copies[step].wait()
        up_copies[step].wait()
        gate = jnp.dot(rows_ref[...], gate_ref[:, at], preferred_element_type=jnp.float32)
        up = jnp.dot(rows_ref[...], up_ref[:, at], preferred_element_type=jnp.float32)
        act_ref[:, at] = (gate / (1.0 + jnp.exp(-gate)) * up).astype(jnp.bfloat16)
    for step in range(out_steps):
        at = columns(step, OUT_CHUNK)
        down_copies[step].wait()
        out = jnp.dot(act_ref[...], down_ref[:, at], preferred_element_type=jnp.float32)
        for piece in range(count):
            out_refs[piece][:, at] = out[piece * depth : (piece + 1) * depth].astype(jnp.bfloat16)


def stream_ffn(pieces, *weights):
    count = len(pieces)
    depth, features = pieces[0].shape
    units = weights[0].shape[1]
    vmem = pl.BlockSpec(memory_space=pltpu.VMEM)
    hbm = pl.BlockSpec(memory_space=pltpu.HBM)
    return pl.pallas_call(
        functools.partial(stream_ffn_kernel, count),
        out_shape=[jax.ShapeDtypeStruct((depth, features), jnp.bfloat16)] * count,
        in_specs=[vmem] * count + [hbm] * 3,
        out_specs=[vmem] * count,
        scratch_shapes=[
            pltpu.VMEM((count * depth, features), jnp.bfloat16),
            pltpu.VMEM((count * depth, units), jnp.bfloat16),
            pltpu.VMEM((features, units), jnp.bfloat16),
            pltpu.VMEM((features, units), jnp.bfloat16),
            pltpu.VMEM((units, features), jnp.bfloat16),
            pltpu.SemaphoreType.DMA((units // UNIT_CHUNK,)),
            pltpu.SemaphoreType.DMA((units // UNIT_CHUNK,)),
            pltpu.SemaphoreType.DMA((features // OUT_CHUNK,)),
        ],
        compiler_params=pltpu.CompilerParams(vmem_limit_bytes=40 << 20),
        cost_estimate=pl.CostEstimate(
            flops=6 * count * depth * features * units,
            transcendentals=count * depth * units,
            bytes_accessed=6 * features * units + 4 * count * depth * features,
        ),
    )(*pieces, *(pltpu.with_memory_space_constraint(w, pltpu.HBM) for w in weights))


def body(
    attn_out,
    residual,
    proj_weight,
    norm_gain,
    gate_weight,
    up_weight,
    down_weight,
    routes,
    route_weights,
):
    model_parts = lax.axis_size("mp")
    unit_parts = lax.axis_size("expert")
    row_count = residual.shape[0]
    features = residual.shape[1]
    def shift(value, by):
        return lax.ppermute(
            value, "expert", [(i, (i + by) % unit_parts) for i in range(unit_parts)]
        )

    expert_ids = routes.reshape(-1)
    onehot = (expert_ids[:, None] == jnp.arange(EXPERTS, dtype=jnp.int32)[None, :]).astype(
        jnp.int32
    )
    before = jnp.cumsum(onehot, axis=0) - onehot
    position = jnp.sum(before * onehot, axis=1)
    target = (expert_ids * MOST + position).reshape(row_count, 2)
    far_target = shift(target, 2)
    residual, far_target = lax.optimization_barrier((residual, far_target))
    blocks = attn_out.reshape(model_parts, unit_parts, row_count, attn_out.shape[1])
    picked = lax.dynamic_index_in_dim(blocks, lax.axis_index("expert"), axis=1, keepdims=False)
    picked = picked.reshape(model_parts * row_count, attn_out.shape[1])
    parts = jnp.dot(picked, proj_weight, preferred_element_type=jnp.float32).astype(jnp.float16)
    parts = parts.reshape(model_parts, row_count, features)
    parts = lax.all_to_all(parts, "mp", split_axis=0, concat_axis=0, tiled=True)
    hidden_state = residual + jnp.sum(parts, axis=0, dtype=jnp.float32)
    inverse_rms = lax.rsqrt(jnp.mean(hidden_state * hidden_state, axis=1, keepdims=True) + EPSILON)
    normed = (hidden_state * inverse_rms * norm_gain).astype(jnp.bfloat16)
    slots = jnp.arange(EXPERTS * MOST, dtype=jnp.int32)

    def chosen(slot_of):
        return slot_of[:, 0][:, None] == slots[None, :], slot_of[:, 1][:, None] == slots[None, :]

    def pack(pair, rows):
        placement = (pair[0] | pair[1]).astype(jnp.bfloat16)
        packed = lax.dot_general(
            placement, rows, (((0,), (0,)), ((), ())), preferred_element_type=jnp.float32
        ).astype(jnp.bfloat16)
        return packed.reshape(model_parts, MOST, features)

    def to_experts(packed):
        packed = lax.all_to_all(packed, "mp", split_axis=0, concat_axis=0, tiled=True)
        return packed.reshape(model_parts * MOST, features)

    first, second = chosen(target)
    far_normed = shift(normed, 2)
    own = to_experts(pack((first, second), normed))
    far_rows = to_experts(pack(chosen(far_target), far_normed))
    stored = (gate_weight[0], up_weight[0], down_weight[0])
    weights = load(*stored)
    before_rows = shift(own, 1)
    after_rows = shift(own, -1)
    (own_sum,) = ffn([own], *weights)
    before_rows, own_sum = lax.optimization_barrier((before_rows, own_sum))
    before_sum, after_sum = ffn([before_rows, after_rows], *weights)
    back_after = shift(before_sum, -1)
    back_before = shift(after_sum, 1)
    far_rows = lax.optimization_barrier((far_rows, before_sum))[0]
    (far_sum,) = stream_ffn([far_rows], *stored)
    back_far = shift(far_sum, 2)
    near = own_sum.astype(jnp.float32)
    near = near + back_after.astype(jnp.float32) + back_before.astype(jnp.float32)
    outputs = lax.optimization_barrier(near) + back_far.astype(jnp.float32)
    outputs = outputs.astype(jnp.bfloat16).reshape(model_parts, MOST, features)
    outputs = lax.all_to_all(outputs, "mp", split_axis=0, concat_axis=0, tiled=True)
    expert_out = outputs.reshape(EXPERTS * MOST, features)
    one = jnp.dot(first.astype(jnp.bfloat16), expert_out, preferred_element_type=jnp.float32)
    two = jnp.dot(second.astype(jnp.bfloat16), expert_out, preferred_element_type=jnp.float32)
    return hidden_state + route_weights[:, 0:1] * one + route_weights[:, 1:2] * two


def solution(mesh):
    in_specs = (
        P("dp", "mp"),
        P(("dp", "mp", "expert"), None),
        P("mp", None),
        P(),
        P("mp", None, "expert"),
        P("mp", None, "expert"),
        P("mp", "expert", None),
        P(("dp", "mp", "expert"), None),
        P(("dp", "mp", "expert"), None),
    )
    out_specs = P(("dp", "mp", "expert"), None)
    return jax.shard_map(body, mesh=mesh, in_specs=in_specs, out_specs=out_specs, check_vma=False)
```

```python
import functools

import jax
import jax.numpy as jnp
from jax import lax
from jax.experimental import pallas as pl
from jax.experimental.pallas import tpu as pltpu
from jax.sharding import PartitionSpec as P

EXPERTS = 8
MOST = 16
EPSILON = 1e-06

UNIT_CHUNK = 512
OUT_CHUNK = 1152


def load_kernel(*refs):
    count = (len(refs) - 1) // 2
    sems = refs[-1]
    copies = [
        pltpu.make_async_copy(refs[i], refs[count + i], sems.at[i]) for i in range(count)
    ]
    for copy in copies:
        copy.start()
    for copy in copies:
        copy.wait()


def load(*weights):
    hbm = pl.BlockSpec(memory_space=pltpu.HBM)
    vmem = pl.BlockSpec(memory_space=pltpu.VMEM)
    total = sum(w.size * w.dtype.itemsize for w in weights)
    return pl.pallas_call(
        load_kernel,
        out_shape=[pltpu.VMEM(w.shape, w.dtype) for w in weights],
        in_specs=[hbm] * len(weights),
        out_specs=[vmem] * len(weights),
        scratch_shapes=[pltpu.SemaphoreType.DMA((len(weights),))],
        compiler_params=pltpu.CompilerParams(vmem_limit_bytes=20 << 20),
        cost_estimate=pl.CostEstimate(flops=0, transcendentals=0, bytes_accessed=2 * total),
    )(*(pltpu.with_memory_space_constraint(w, pltpu.HBM) for w in weights))


def ffn_kernel(count, *refs):
    row_refs, refs = refs[:count], refs[count:]
    (gate_ref, up_ref, down_ref), refs = refs[:3], refs[3:]
    out_refs, refs = refs[:count], refs[count:]
    act_ref = refs[0]
    depth = row_refs[0].shape[0]
    if count == 1:
        rows_ref = row_refs[0]
    else:
        rows_ref = refs[1]
        for piece in range(count):
            rows_ref[pl.ds(piece * depth, depth), :] = row_refs[piece][...]
    for start in range(0, act_ref.shape[1], UNIT_CHUNK):
        at = pl.ds(start, UNIT_CHUNK)
        gate = jnp.dot(rows_ref[...], gate_ref[:, at], preferred_element_type=jnp.float32)
        up = jnp.dot(rows_ref[...], up_ref[:, at], preferred_element_type=jnp.float32)
        act_ref[:, at] = (gate / (1.0 + jnp.exp(-gate)) * up).astype(jnp.bfloat16)
    for start in range(0, down_ref.shape[1], OUT_CHUNK):
        at = pl.ds(start, OUT_CHUNK)
        out = jnp.dot(act_ref[...], down_ref[:, at], preferred_element_type=jnp.float32)
        for piece in range(count):
            out_refs[piece][:, at] = out[piece * depth : (piece + 1) * depth].astype(jnp.bfloat16)


def ffn(pieces, *weights):
    count = len(pieces)
    depth, features = pieces[0].shape
    units = weights[0].shape[1]
    vmem = pl.BlockSpec(memory_space=pltpu.VMEM)
    scratch = [pltpu.VMEM((count * depth, units), jnp.bfloat16)]
    if count > 1:
        scratch.append(pltpu.VMEM((count * depth, features), jnp.bfloat16))
    return pl.pallas_call(
        functools.partial(ffn_kernel, count),
        out_shape=[jax.ShapeDtypeStruct((depth, features), jnp.bfloat16)] * count,
        in_specs=[vmem] * (count + 3),
        out_specs=[vmem] * count,
        scratch_shapes=scratch,
        compiler_params=pltpu.CompilerParams(vmem_limit_bytes=24 << 20),
        cost_estimate=pl.CostEstimate(
            flops=6 * count * depth * features * units,
            transcendentals=count * depth * units,
            bytes_accessed=6 * features * units + 4 * count * depth * features,
        ),
    )(*pieces, *weights)


def body(
    attn_out,
    residual,
    proj_weight,
    norm_gain,
    gate_weight,
    up_weight,
    down_weight,
    routes,
    route_weights,
):
    model_parts = lax.axis_size("mp")
    unit_parts = lax.axis_size("expert")
    row_count = residual.shape[0]
    features = residual.shape[1]
    def shift(value, by):
        return lax.ppermute(
            value, "expert", [(i, (i + by) % unit_parts) for i in range(unit_parts)]
        )

    expert_ids = routes.reshape(-1)
    onehot = (expert_ids[:, None] == jnp.arange(EXPERTS, dtype=jnp.int32)[None, :]).astype(
        jnp.int32
    )
    before = jnp.cumsum(onehot, axis=0) - onehot
    position = jnp.sum(before * onehot, axis=1)
    target = (expert_ids * MOST + position).reshape(row_count, 2)
    far_routing = jnp.concatenate([target.astype(jnp.float32), route_weights], axis=1)
    far_routing = shift(far_routing, 2)
    residual, far_routing = lax.optimization_barrier((residual, far_routing))
    blocks = attn_out.reshape(model_parts, unit_parts, row_count, attn_out.shape[1])
    picked = lax.dynamic_index_in_dim(blocks, lax.axis_index("expert"), axis=1, keepdims=False)
    picked = picked.reshape(model_parts * row_count, attn_out.shape[1])
    parts = jnp.dot(picked, proj_weight, preferred_element_type=jnp.float32).astype(jnp.float16)
    parts = parts.reshape(model_parts, row_count, features)
    parts = lax.all_to_all(parts, "mp", split_axis=0, concat_axis=0, tiled=True)
    hidden_state = residual + jnp.sum(parts, axis=0, dtype=jnp.float32)
    inverse_rms = lax.rsqrt(jnp.mean(hidden_state * hidden_state, axis=1, keepdims=True) + EPSILON)
    normed = (hidden_state * inverse_rms * norm_gain).astype(jnp.bfloat16)
    slots = jnp.arange(EXPERTS * MOST, dtype=jnp.int32)

    def chosen(slot_of):
        return slot_of[:, 0][:, None] == slots[None, :], slot_of[:, 1][:, None] == slots[None, :]

    def weighted(pair, weight_of, sums):
        one = jnp.dot(pair[0].astype(jnp.bfloat16), sums, preferred_element_type=jnp.float32)
        two = jnp.dot(pair[1].astype(jnp.bfloat16), sums, preferred_element_type=jnp.float32)
        return weight_of[:, 0:1] * one + weight_of[:, 1:2] * two

    first, second = chosen(target)
    placement = (first | second).astype(jnp.bfloat16)
    outgoing = lax.dot_general(
        placement, normed, (((0,), (0,)), ((), ())), preferred_element_type=jnp.float32
    ).astype(jnp.bfloat16)
    outgoing = outgoing.reshape(model_parts, MOST, features)
    arrived = lax.all_to_all(outgoing, "mp", split_axis=0, concat_axis=0, tiled=True)
    own = arrived.reshape(model_parts * MOST, features)

    weights = load(gate_weight[0], up_weight[0], down_weight[0])

    before_rows = shift(own, 1)
    after_rows = shift(own, -1)
    (own_sum,) = ffn([own], *weights)
    far_rows = shift(lax.optimization_barrier((own, own_sum))[0], 2)
    before_sum, after_sum = ffn([before_rows, after_rows], *weights)
    back_after = shift(before_sum, -1)
    back_before = shift(after_sum, 1)
    far_rows = lax.optimization_barrier((far_rows, before_sum))[0]
    (far_sum,) = ffn([far_rows], *weights)
    far_sums = lax.all_to_all(
        far_sum.reshape(model_parts, MOST, features), "mp", split_axis=0, concat_axis=0, tiled=True
    )
    near = own_sum.astype(jnp.float32)
    near = near + back_after.astype(jnp.float32) + back_before.astype(jnp.float32)
    near = near.astype(jnp.bfloat16).reshape(model_parts, MOST, features)
    near, far_sums = lax.optimization_barrier((near, far_sums))
    near = lax.all_to_all(near, "mp", split_axis=0, concat_axis=0, tiled=True)
    far_part = weighted(
        chosen(far_routing[:, 0:2].astype(jnp.int32)),
        far_routing[:, 2:4],
        far_sums.reshape(EXPERTS * MOST, features),
    )
    far_part = shift(far_part, 2)
    near_part = weighted((first, second), route_weights, near.reshape(EXPERTS * MOST, features))
    return hidden_state + near_part + far_part


def solution(mesh):
    in_specs = (
        P("dp", "mp"),
        P(("dp", "mp", "expert"), None),
        P("mp", None),
        P(),
        P("mp", None, "expert"),
        P("mp", None, "expert"),
        P("mp", "expert", None),
        P(("dp", "mp", "expert"), None),
        P(("dp", "mp", "expert"), None),
    )
    out_specs = P(("dp", "mp", "expert"), None)
    return jax.shard_map(body, mesh=mesh, in_specs=in_specs, out_specs=out_specs, check_vma=False)
```

```python
import functools

import jax
import jax.numpy as jnp
from jax import lax
from jax.experimental import pallas as pl
from jax.experimental.pallas import tpu as pltpu
from jax.sharding import PartitionSpec as P

EXPERTS = 8
MOST = 16
HALF = 8
EPSILON = 1e-06

UNIT_CHUNK = 512
OUT_CHUNK = 1152


def load_kernel(*refs):
    count = (len(refs) - 1) // 2
    sems = refs[-1]
    copies = [
        pltpu.make_async_copy(refs[i], refs[count + i], sems.at[i]) for i in range(count)
    ]
    for copy in copies:
        copy.start()
    for copy in copies:
        copy.wait()


def load(*weights):
    hbm = pl.BlockSpec(memory_space=pltpu.HBM)
    vmem = pl.BlockSpec(memory_space=pltpu.VMEM)
    total = sum(w.size * w.dtype.itemsize for w in weights)
    return pl.pallas_call(
        load_kernel,
        out_shape=[pltpu.VMEM(w.shape, w.dtype) for w in weights],
        in_specs=[hbm] * len(weights),
        out_specs=[vmem] * len(weights),
        scratch_shapes=[pltpu.SemaphoreType.DMA((len(weights),))],
        compiler_params=pltpu.CompilerParams(vmem_limit_bytes=20 << 20),
        cost_estimate=pl.CostEstimate(flops=0, transcendentals=0, bytes_accessed=2 * total),
    )(*(pltpu.with_memory_space_constraint(w, pltpu.HBM) for w in weights))


def ffn_kernel(count, halves, *refs):
    row_refs, refs = refs[:count], refs[count:]
    (gate_ref, up_ref, down_ref), refs = refs[:3], refs[3:]
    out_refs, refs = refs[: 2 if halves else count], refs[2 if halves else count :]
    act_ref = refs[0]
    depth = row_refs[0].shape[0]
    if count == 1:
        rows_ref = row_refs[0]
    else:
        rows_ref = refs[1]
        for piece in range(count):
            rows_ref[pl.ds(piece * depth, depth), :] = row_refs[piece][...]
    for start in range(0, act_ref.shape[1], UNIT_CHUNK):
        at = pl.ds(start, UNIT_CHUNK)
        gate = jnp.dot(rows_ref[...], gate_ref[:, at], preferred_element_type=jnp.float32)
        up = jnp.dot(rows_ref[...], up_ref[:, at], preferred_element_type=jnp.float32)
        act_ref[:, at] = (gate / (1.0 + jnp.exp(-gate)) * up).astype(jnp.bfloat16)
    for start in range(0, down_ref.shape[1], OUT_CHUNK):
        at = pl.ds(start, OUT_CHUNK)
        out = jnp.dot(act_ref[...], down_ref[:, at], preferred_element_type=jnp.float32)
        if halves:
            for block in range(depth // HALF):
                rows = out[block * HALF : (block + 1) * HALF].astype(jnp.bfloat16)
                out_refs[block % 2][pl.ds(block // 2 * HALF, HALF), at] = rows
            continue
        for piece in range(count):
            out_refs[piece][:, at] = out[piece * depth : (piece + 1) * depth].astype(jnp.bfloat16)


def ffn(pieces, *weights, halves=False):
    count = len(pieces)
    depth, features = pieces[0].shape
    units = weights[0].shape[1]
    vmem = pl.BlockSpec(memory_space=pltpu.VMEM)
    scratch = [pltpu.VMEM((count * depth, units), jnp.bfloat16)]
    if count > 1:
        scratch.append(pltpu.VMEM((count * depth, features), jnp.bfloat16))
    return pl.pallas_call(
        functools.partial(ffn_kernel, count, halves),
        out_shape=[jax.ShapeDtypeStruct((depth // 2 if halves else depth, features), jnp.bfloat16)]
        * (2 if halves else count),
        in_specs=[vmem] * (count + 3),
        out_specs=[vmem] * (2 if halves else count),
        scratch_shapes=scratch,
        compiler_params=pltpu.CompilerParams(vmem_limit_bytes=24 << 20),
        cost_estimate=pl.CostEstimate(
            flops=6 * count * depth * features * units,
            transcendentals=count * depth * units,
            bytes_accessed=6 * features * units + 4 * count * depth * features,
        ),
    )(*pieces, *weights)


def body(
    attn_out,
    residual,
    proj_weight,
    norm_gain,
    gate_weight,
    up_weight,
    down_weight,
    routes,
    route_weights,
):
    model_parts = lax.axis_size("mp")
    unit_parts = lax.axis_size("expert")
    row_count = residual.shape[0]
    features = residual.shape[1]
    def shift(value, by):
        return lax.ppermute(
            value, "expert", [(i, (i + by) % unit_parts) for i in range(unit_parts)]
        )

    expert_ids = routes.reshape(-1)
    onehot = (expert_ids[:, None] == jnp.arange(EXPERTS, dtype=jnp.int32)[None, :]).astype(
        jnp.int32
    )
    before = jnp.cumsum(onehot, axis=0) - onehot
    position = jnp.sum(before * onehot, axis=1)
    target = (expert_ids * MOST + position).reshape(row_count, 2)
    far_routing = jnp.concatenate([target.astype(jnp.float32), route_weights], axis=1)
    far_routing = shift(far_routing, 2)
    slots = jnp.arange(EXPERTS * MOST, dtype=jnp.int32)
    late_slots = slots.reshape(EXPERTS, MOST)[:, HALF:].reshape(-1)

    def chosen(slot_of, among):
        return slot_of[:, 0][:, None] == among[None, :], slot_of[:, 1][:, None] == among[None, :]

    far_pair = chosen(far_routing[:, 0:2].astype(jnp.int32), late_slots)
    far_pair = tuple(value.astype(jnp.bfloat16) for value in far_pair)
    far_weights = far_routing[:, 2:4]
    residual, far_pair, far_weights = lax.optimization_barrier((residual, far_pair, far_weights))
    blocks = attn_out.reshape(model_parts, unit_parts, row_count, attn_out.shape[1])
    picked = lax.dynamic_index_in_dim(blocks, lax.axis_index("expert"), axis=1, keepdims=False)
    picked = picked.reshape(model_parts * row_count, attn_out.shape[1])
    parts = jnp.dot(picked, proj_weight, preferred_element_type=jnp.float32).astype(jnp.float16)
    parts = parts.reshape(model_parts, row_count, features)
    parts = lax.all_to_all(parts, "mp", split_axis=0, concat_axis=0, tiled=True)
    hidden_state = residual + jnp.sum(parts, axis=0, dtype=jnp.float32)
    inverse_rms = lax.rsqrt(jnp.mean(hidden_state * hidden_state, axis=1, keepdims=True) + EPSILON)
    normed = (hidden_state * inverse_rms * norm_gain).astype(jnp.bfloat16)

    def weighted(pair, weight_of, sums):
        one = jnp.dot(pair[0].astype(jnp.bfloat16), sums, preferred_element_type=jnp.float32)
        two = jnp.dot(pair[1].astype(jnp.bfloat16), sums, preferred_element_type=jnp.float32)
        return weight_of[:, 0:1] * one + weight_of[:, 1:2] * two

    first, second = chosen(target, slots)
    placement = (first | second).astype(jnp.bfloat16)
    outgoing = lax.dot_general(
        placement, normed, (((0,), (0,)), ((), ())), preferred_element_type=jnp.float32
    ).astype(jnp.bfloat16)
    outgoing = outgoing.reshape(model_parts, MOST, features)
    arrived = lax.all_to_all(outgoing, "mp", split_axis=0, concat_axis=0, tiled=True)
    own = arrived.reshape(model_parts * MOST, features)

    weights = load(gate_weight[0], up_weight[0], down_weight[0])

    before_rows = shift(own, 1)
    after_rows = shift(own, -1)
    (own_sum,) = ffn([own], *weights)
    far_rows = shift(lax.optimization_barrier((own, own_sum))[0], 2)
    before_sum, after_sum = ffn([before_rows, after_rows], *weights)
    back_after = shift(before_sum, -1)
    back_before = shift(after_sum, 1)
    far_rows = lax.optimization_barrier((far_rows, before_sum))[0]
    far_sum, late_sum = ffn([far_rows], *weights, halves=True)
    late_sum = late_sum.reshape(model_parts, MOST - HALF, features)
    far_sums = lax.all_to_all(late_sum, "mp", split_axis=0, concat_axis=0, tiled=True)
    back_far = shift(far_sum, 2).reshape(model_parts, HALF, features)
    near = own_sum.astype(jnp.float32)
    near = near + back_after.astype(jnp.float32) + back_before.astype(jnp.float32)
    near = lax.optimization_barrier(near).reshape(model_parts, MOST, features)
    near = jnp.concatenate([near[:, :HALF] + back_far.astype(jnp.float32), near[:, HALF:]], axis=1)
    near = near.astype(jnp.bfloat16)
    near, far_sums = lax.optimization_barrier((near, far_sums))
    near = lax.all_to_all(near, "mp", split_axis=0, concat_axis=0, tiled=True)
    far_part = weighted(
        far_pair,
        far_weights,
        far_sums.reshape(EXPERTS * (MOST - HALF), features),
    )
    far_part = shift(far_part, 2)
    near_part = weighted((first, second), route_weights, near.reshape(EXPERTS * MOST, features))
    return hidden_state + near_part + far_part


def solution(mesh):
    in_specs = (
        P("dp", "mp"),
        P(("dp", "mp", "expert"), None),
        P("mp", None),
        P(),
        P("mp", None, "expert"),
        P("mp", None, "expert"),
        P("mp", "expert", None),
        P(("dp", "mp", "expert"), None),
        P(("dp", "mp", "expert"), None),
    )
    out_specs = P(("dp", "mp", "expert"), None)
    return jax.shard_map(body, mesh=mesh, in_specs=in_specs, out_specs=out_specs, check_vma=False)
```

```python
import functools

import jax
import jax.numpy as jnp
from jax import lax
from jax.experimental import pallas as pl
from jax.experimental.pallas import tpu as pltpu
from jax.sharding import PartitionSpec as P

EXPERTS = 8
MOST = 16
HALF = 8
EPSILON = 1e-06

UNIT_CHUNK = 512
OUT_CHUNK = 1152


def load_kernel(*refs):
    count = (len(refs) - 1) // 2
    sems = refs[-1]
    copies = [
        pltpu.make_async_copy(refs[i], refs[count + i], sems.at[i]) for i in range(count)
    ]
    for copy in copies:
        copy.start()
    for copy in copies:
        copy.wait()


def load(*weights):
    hbm = pl.BlockSpec(memory_space=pltpu.HBM)
    vmem = pl.BlockSpec(memory_space=pltpu.VMEM)
    total = sum(w.size * w.dtype.itemsize for w in weights)
    return pl.pallas_call(
        load_kernel,
        out_shape=[pltpu.VMEM(w.shape, w.dtype) for w in weights],
        in_specs=[hbm] * len(weights),
        out_specs=[vmem] * len(weights),
        scratch_shapes=[pltpu.SemaphoreType.DMA((len(weights),))],
        compiler_params=pltpu.CompilerParams(vmem_limit_bytes=20 << 20),
        cost_estimate=pl.CostEstimate(flops=0, transcendentals=0, bytes_accessed=2 * total),
    )(*(pltpu.with_memory_space_constraint(w, pltpu.HBM) for w in weights))


def ffn_kernel(count, halves, *refs):
    row_refs, refs = refs[:count], refs[count:]
    (gate_ref, up_ref, down_ref), refs = refs[:3], refs[3:]
    out_refs, refs = refs[: 2 if halves else count], refs[2 if halves else count :]
    act_ref = refs[0]
    depth = row_refs[0].shape[0]
    if count == 1:
        rows_ref = row_refs[0]
    else:
        rows_ref = refs[1]
        for piece in range(count):
            rows_ref[pl.ds(piece * depth, depth), :] = row_refs[piece][...]
    for start in range(0, act_ref.shape[1], UNIT_CHUNK):
        at = pl.ds(start, UNIT_CHUNK)
        gate = jnp.dot(rows_ref[...], gate_ref[:, at], preferred_element_type=jnp.float32)
        up = jnp.dot(rows_ref[...], up_ref[:, at], preferred_element_type=jnp.float32)
        act_ref[:, at] = (gate / (1.0 + jnp.exp(-gate)) * up).astype(jnp.bfloat16)
    for start in range(0, down_ref.shape[1], OUT_CHUNK):
        at = pl.ds(start, OUT_CHUNK)
        out = jnp.dot(act_ref[...], down_ref[:, at], preferred_element_type=jnp.float32)
        if halves:
            for block in range(depth // HALF):
                rows = out[block * HALF : (block + 1) * HALF].astype(jnp.bfloat16)
                out_refs[block % 2][pl.ds(block // 2 * HALF, HALF), at] = rows
            continue
        for piece in range(count):
            out_refs[piece][:, at] = out[piece * depth : (piece + 1) * depth].astype(jnp.bfloat16)


def ffn(pieces, *weights, halves=False):
    count = len(pieces)
    depth, features = pieces[0].shape
    units = weights[0].shape[1]
    vmem = pl.BlockSpec(memory_space=pltpu.VMEM)
    scratch = [pltpu.VMEM((count * depth, units), jnp.bfloat16)]
    if count > 1:
        scratch.append(pltpu.VMEM((count * depth, features), jnp.bfloat16))
    return pl.pallas_call(
        functools.partial(ffn_kernel, count, halves),
        out_shape=[jax.ShapeDtypeStruct((depth // 2 if halves else depth, features), jnp.bfloat16)]
        * (2 if halves else count),
        in_specs=[vmem] * (count + 3),
        out_specs=[vmem] * (2 if halves else count),
        scratch_shapes=scratch,
        compiler_params=pltpu.CompilerParams(vmem_limit_bytes=24 << 20),
        cost_estimate=pl.CostEstimate(
            flops=6 * count * depth * features * units,
            transcendentals=count * depth * units,
            bytes_accessed=6 * features * units + 4 * count * depth * features,
        ),
    )(*pieces, *weights)


def body(
    attn_out,
    residual,
    proj_weight,
    norm_gain,
    gate_weight,
    up_weight,
    down_weight,
    routes,
    route_weights,
):
    model_parts = lax.axis_size("mp")
    unit_parts = lax.axis_size("expert")
    row_count = residual.shape[0]
    features = residual.shape[1]
    def shift(value, by):
        return lax.ppermute(
            value, "expert", [(i, (i + by) % unit_parts) for i in range(unit_parts)]
        )

    expert_ids = routes.reshape(-1)
    onehot = (expert_ids[:, None] == jnp.arange(EXPERTS, dtype=jnp.int32)[None, :]).astype(
        jnp.int32
    )
    before = jnp.cumsum(onehot, axis=0) - onehot
    position = jnp.sum(before * onehot, axis=1)
    target = (expert_ids * MOST + position).reshape(row_count, 2)
    far_routing = jnp.concatenate([target.astype(jnp.float32), route_weights], axis=1)
    far_routing = shift(far_routing, 2)
    slots = jnp.arange(EXPERTS * MOST, dtype=jnp.int32)
    late_slots = slots.reshape(EXPERTS, MOST)[:, HALF:].reshape(-1)

    def chosen(slot_of, among):
        return slot_of[:, 0][:, None] == among[None, :], slot_of[:, 1][:, None] == among[None, :]

    far_pair = chosen(far_routing[:, 0:2].astype(jnp.int32), late_slots)
    far_pair = tuple(value.astype(jnp.bfloat16) for value in far_pair)
    far_weights = far_routing[:, 2:4]
    residual, far_pair, far_weights = lax.optimization_barrier((residual, far_pair, far_weights))
    blocks = attn_out.reshape(model_parts, unit_parts, row_count, attn_out.shape[1])
    picked = lax.dynamic_index_in_dim(blocks, lax.axis_index("expert"), axis=1, keepdims=False)
    picked = picked.reshape(model_parts * row_count, attn_out.shape[1])
    parts = jnp.dot(picked, proj_weight, preferred_element_type=jnp.float32).astype(jnp.float16)
    parts = parts.reshape(model_parts, row_count, features)
    parts = lax.all_to_all(parts, "mp", split_axis=0, concat_axis=0, tiled=True)
    hidden_state = residual + jnp.sum(parts, axis=0, dtype=jnp.float32)
    inverse_rms = lax.rsqrt(jnp.mean(hidden_state * hidden_state, axis=1, keepdims=True) + EPSILON)
    normed = (hidden_state * inverse_rms * norm_gain).astype(jnp.bfloat16)

    def weighted(pair, weight_of, sums):
        one = jnp.dot(pair[0].astype(jnp.bfloat16), sums, preferred_element_type=jnp.float32)
        two = jnp.dot(pair[1].astype(jnp.bfloat16), sums, preferred_element_type=jnp.float32)
        return weight_of[:, 0:1] * one + weight_of[:, 1:2] * two

    first, second = chosen(target, slots)
    placement = (first | second).astype(jnp.bfloat16)
    outgoing = lax.dot_general(
        placement, normed, (((0,), (0,)), ((), ())), preferred_element_type=jnp.float32
    ).astype(jnp.bfloat16)
    outgoing = outgoing.reshape(model_parts, MOST, features)
    arrived = lax.all_to_all(outgoing, "mp", split_axis=0, concat_axis=0, tiled=True)
    own = arrived.reshape(model_parts * MOST, features)

    weights = load(gate_weight[0], up_weight[0], down_weight[0])

    before_rows = shift(own, 1)
    after_rows = shift(own, -1)
    (own_sum,) = ffn([own], *weights)
    later, before_rows, after_rows, own_sum = lax.optimization_barrier(
        (own, before_rows, after_rows, own_sum)
    )
    far_rows = shift(later, 2)
    before_sum, after_sum = ffn([before_rows, after_rows], *weights)
    back_after = shift(before_sum, -1)
    back_before = shift(after_sum, 1)
    far_rows = lax.optimization_barrier((far_rows, before_sum))[0]
    far_sum, late_sum = ffn([far_rows], *weights, halves=True)
    late_sum = late_sum.reshape(model_parts, MOST - HALF, features)
    far_sums = lax.all_to_all(late_sum, "mp", split_axis=0, concat_axis=0, tiled=True)
    back_far = shift(far_sum, 2)
    far_sums, back_far = lax.optimization_barrier((far_sums, back_far))
    back_far = back_far.reshape(model_parts, HALF, features)
    near = own_sum.astype(jnp.float32)
    near = near + back_after.astype(jnp.float32) + back_before.astype(jnp.float32)
    near = lax.optimization_barrier(near).reshape(model_parts, MOST, features)
    near = jnp.concatenate([near[:, :HALF] + back_far.astype(jnp.float32), near[:, HALF:]], axis=1)
    near = near.astype(jnp.bfloat16)
    near, far_sums = lax.optimization_barrier((near, far_sums))
    near = lax.all_to_all(near, "mp", split_axis=0, concat_axis=0, tiled=True)
    far_part = weighted(
        far_pair,
        far_weights,
        far_sums.reshape(EXPERTS * (MOST - HALF), features),
    )
    far_part = shift(far_part, 2)
    near_part = weighted((first, second), route_weights, near.reshape(EXPERTS * MOST, features))
    return hidden_state + near_part + far_part


def solution(mesh):
    in_specs = (
        P("dp", "mp"),
        P(("dp", "mp", "expert"), None),
        P("mp", None),
        P(),
        P("mp", None, "expert"),
        P("mp", None, "expert"),
        P("mp", "expert", None),
        P(("dp", "mp", "expert"), None),
        P(("dp", "mp", "expert"), None),
    )
    out_specs = P(("dp", "mp", "expert"), None)
    return jax.shard_map(body, mesh=mesh, in_specs=in_specs, out_specs=out_specs, check_vma=False)
```

```python
import functools

import jax
import jax.numpy as jnp
from jax import lax
from jax.experimental import pallas as pl
from jax.experimental.pallas import tpu as pltpu
from jax.sharding import PartitionSpec as P

EXPERTS = 8
MOST = 16
EPSILON = 1e-06

UNIT_CHUNK = 512
OUT_CHUNK = 1152


def load_kernel(*refs):
    count = (len(refs) - 1) // 2
    sems = refs[-1]
    copies = [
        pltpu.make_async_copy(refs[i], refs[count + i], sems.at[i]) for i in range(count)
    ]
    for copy in copies:
        copy.start()
    for copy in copies:
        copy.wait()


def load(*weights):
    hbm = pl.BlockSpec(memory_space=pltpu.HBM)
    vmem = pl.BlockSpec(memory_space=pltpu.VMEM)
    total = sum(w.size * w.dtype.itemsize for w in weights)
    return pl.pallas_call(
        load_kernel,
        out_shape=[pltpu.VMEM(w.shape, w.dtype) for w in weights],
        in_specs=[hbm] * len(weights),
        out_specs=[vmem] * len(weights),
        scratch_shapes=[pltpu.SemaphoreType.DMA((len(weights),))],
        compiler_params=pltpu.CompilerParams(vmem_limit_bytes=20 << 20),
        cost_estimate=pl.CostEstimate(flops=0, transcendentals=0, bytes_accessed=2 * total),
    )(*(pltpu.with_memory_space_constraint(w, pltpu.HBM) for w in weights))


def ffn_kernel(count, *refs):
    row_refs, refs = refs[:count], refs[count:]
    (gate_ref, up_ref, down_ref), refs = refs[:3], refs[3:]
    out_refs, refs = refs[:count], refs[count:]
    act_ref = refs[0]
    depth = row_refs[0].shape[0]
    if count == 1:
        rows_ref = row_refs[0]
    else:
        rows_ref = refs[1]
        for piece in range(count):
            rows_ref[pl.ds(piece * depth, depth), :] = row_refs[piece][...]
    for start in range(0, act_ref.shape[1], UNIT_CHUNK):
        at = pl.ds(start, UNIT_CHUNK)
        gate = jnp.dot(rows_ref[...], gate_ref[:, at], preferred_element_type=jnp.float32)
        up = jnp.dot(rows_ref[...], up_ref[:, at], preferred_element_type=jnp.float32)
        act_ref[:, at] = (gate / (1.0 + jnp.exp(-gate)) * up).astype(jnp.bfloat16)
    for start in range(0, down_ref.shape[1], OUT_CHUNK):
        at = pl.ds(start, OUT_CHUNK)
        out = jnp.dot(act_ref[...], down_ref[:, at], preferred_element_type=jnp.float32)
        for piece in range(count):
            out_refs[piece][:, at] = out[piece * depth : (piece + 1) * depth].astype(jnp.bfloat16)


def ffn(pieces, *weights):
    count = len(pieces)
    depth, features = pieces[0].shape
    units = weights[0].shape[1]
    vmem = pl.BlockSpec(memory_space=pltpu.VMEM)
    scratch = [pltpu.VMEM((count * depth, units), jnp.bfloat16)]
    if count > 1:
        scratch.append(pltpu.VMEM((count * depth, features), jnp.bfloat16))
    return pl.pallas_call(
        functools.partial(ffn_kernel, count),
        out_shape=[jax.ShapeDtypeStruct((depth, features), jnp.bfloat16)] * count,
        in_specs=[vmem] * (count + 3),
        out_specs=[vmem] * count,
        scratch_shapes=scratch,
        compiler_params=pltpu.CompilerParams(vmem_limit_bytes=24 << 20),
        cost_estimate=pl.CostEstimate(
            flops=6 * count * depth * features * units,
            transcendentals=count * depth * units,
            bytes_accessed=6 * features * units + 4 * count * depth * features,
        ),
    )(*pieces, *weights)


def body(
    attn_out,
    residual,
    proj_weight,
    norm_gain,
    gate_weight,
    up_weight,
    down_weight,
    routes,
    route_weights,
):
    model_parts = lax.axis_size("mp")
    unit_parts = lax.axis_size("expert")
    row_count = residual.shape[0]
    features = residual.shape[1]
    blocks = attn_out.reshape(model_parts, unit_parts, row_count, attn_out.shape[1])
    picked = lax.dynamic_index_in_dim(blocks, lax.axis_index("expert"), axis=1, keepdims=False)
    picked = picked.reshape(model_parts * row_count, attn_out.shape[1])
    parts = jnp.dot(picked, proj_weight, preferred_element_type=jnp.float32).astype(jnp.float16)
    parts = parts.reshape(model_parts, row_count, features)
    parts = lax.all_to_all(parts, "mp", split_axis=0, concat_axis=0, tiled=True)
    hidden_state = residual + jnp.sum(parts, axis=0, dtype=jnp.float32)
    inverse_rms = lax.rsqrt(jnp.mean(hidden_state * hidden_state, axis=1, keepdims=True) + EPSILON)
    normed = (hidden_state * inverse_rms * norm_gain).astype(jnp.bfloat16)
    expert_ids = routes.reshape(-1)
    onehot = (expert_ids[:, None] == jnp.arange(EXPERTS, dtype=jnp.int32)[None, :]).astype(
        jnp.int32
    )
    before = jnp.cumsum(onehot, axis=0) - onehot
    position = jnp.sum(before * onehot, axis=1)
    target = (expert_ids * MOST + position).reshape(row_count, 2)
    slots = jnp.arange(EXPERTS * MOST, dtype=jnp.int32)
    first = target[:, 0][:, None] == slots[None, :]
    second = target[:, 1][:, None] == slots[None, :]
    placement = (first | second).astype(jnp.bfloat16)
    outgoing = lax.dot_general(
        placement, normed, (((0,), (0,)), ((), ())), preferred_element_type=jnp.float32
    ).astype(jnp.bfloat16)
    outgoing = outgoing.reshape(model_parts, MOST, features)
    arrived = lax.all_to_all(outgoing, "mp", split_axis=0, concat_axis=0, tiled=True)
    own = arrived.reshape(model_parts * MOST, features)

    weights = load(gate_weight[0], up_weight[0], down_weight[0])

    def shift(value, by):
        return lax.ppermute(
            value, "expert", [(i, (i + by) % unit_parts) for i in range(unit_parts)]
        )

    before_rows = shift(own, 1)
    after_rows = shift(own, -1)
    (own_sum,) = ffn([own], *weights)
    later, before_rows, after_rows, own_sum = lax.optimization_barrier(
        (own, before_rows, after_rows, own_sum)
    )
    far_rows = shift(later, 2)
    before_sum, after_sum = ffn([before_rows, after_rows], *weights)
    back_after = shift(before_sum, -1)
    back_before = shift(after_sum, 1)
    far_rows = lax.optimization_barrier((far_rows, before_sum))[0]
    (far_sum,) = ffn([far_rows], *weights)
    back_far = shift(far_sum, 2)
    near = own_sum.astype(jnp.float32)
    near = near + back_after.astype(jnp.float32) + back_before.astype(jnp.float32)
    outputs = lax.optimization_barrier(near) + back_far.astype(jnp.float32)
    outputs = outputs.astype(jnp.bfloat16).reshape(model_parts, MOST, features)
    outputs = lax.all_to_all(outputs, "mp", split_axis=0, concat_axis=0, tiled=True)
    expert_out = outputs.reshape(EXPERTS * MOST, features)
    one = jnp.dot(first.astype(jnp.bfloat16), expert_out, preferred_element_type=jnp.float32)
    two = jnp.dot(second.astype(jnp.bfloat16), expert_out, preferred_element_type=jnp.float32)
    return hidden_state + route_weights[:, 0:1] * one + route_weights[:, 1:2] * two


def solution(mesh):
    in_specs = (
        P("dp", "mp"),
        P(("dp", "mp", "expert"), None),
        P("mp", None),
        P(),
        P("mp", None, "expert"),
        P("mp", None, "expert"),
        P("mp", "expert", None),
        P(("dp", "mp", "expert"), None),
        P(("dp", "mp", "expert"), None),
    )
    out_specs = P(("dp", "mp", "expert"), None)
    return jax.shard_map(body, mesh=mesh, in_specs=in_specs, out_specs=out_specs, check_vma=False)
```

```python
import functools

import jax
import jax.numpy as jnp
from jax import lax
from jax.experimental import pallas as pl
from jax.experimental.pallas import tpu as pltpu
from jax.sharding import PartitionSpec as P

EXPERTS = 8
MOST = 16
EPSILON = 1e-06

UNIT_CHUNK = 512
OUT_CHUNK = 1152


def load_kernel(*refs):
    count = (len(refs) - 1) // 2
    sems = refs[-1]
    copies = [
        pltpu.make_async_copy(refs[i], refs[count + i], sems.at[i]) for i in range(count)
    ]
    for copy in copies:
        copy.start()
    for copy in copies:
        copy.wait()


def load(*weights):
    hbm = pl.BlockSpec(memory_space=pltpu.HBM)
    vmem = pl.BlockSpec(memory_space=pltpu.VMEM)
    total = sum(w.size * w.dtype.itemsize for w in weights)
    return pl.pallas_call(
        load_kernel,
        out_shape=[pltpu.VMEM(w.shape, w.dtype) for w in weights],
        in_specs=[hbm] * len(weights),
        out_specs=[vmem] * len(weights),
        scratch_shapes=[pltpu.SemaphoreType.DMA((len(weights),))],
        compiler_params=pltpu.CompilerParams(vmem_limit_bytes=20 << 20),
        cost_estimate=pl.CostEstimate(flops=0, transcendentals=0, bytes_accessed=2 * total),
    )(*(pltpu.with_memory_space_constraint(w, pltpu.HBM) for w in weights))


def ffn_kernel(count, *refs):
    row_refs, refs = refs[:count], refs[count:]
    (gate_ref, up_ref, down_ref), refs = refs[:3], refs[3:]
    out_refs, refs = refs[:count], refs[count:]
    act_ref = refs[0]
    depth = row_refs[0].shape[0]
    if count == 1:
        rows_ref = row_refs[0]
    else:
        rows_ref = refs[1]
        for piece in range(count):
            rows_ref[pl.ds(piece * depth, depth), :] = row_refs[piece][...]
    for start in range(0, act_ref.shape[1], UNIT_CHUNK):
        at = pl.ds(start, UNIT_CHUNK)
        gate = jnp.dot(rows_ref[...], gate_ref[:, at], preferred_element_type=jnp.float32)
        up = jnp.dot(rows_ref[...], up_ref[:, at], preferred_element_type=jnp.float32)
        act_ref[:, at] = (gate / (1.0 + jnp.exp(-gate)) * up).astype(jnp.bfloat16)
    for start in range(0, down_ref.shape[1], OUT_CHUNK):
        at = pl.ds(start, OUT_CHUNK)
        out = jnp.dot(act_ref[...], down_ref[:, at], preferred_element_type=jnp.float32)
        for piece in range(count):
            out_refs[piece][:, at] = out[piece * depth : (piece + 1) * depth].astype(jnp.bfloat16)


def ffn(pieces, *weights):
    count = len(pieces)
    depth, features = pieces[0].shape
    units = weights[0].shape[1]
    vmem = pl.BlockSpec(memory_space=pltpu.VMEM)
    scratch = [pltpu.VMEM((count * depth, units), jnp.bfloat16)]
    if count > 1:
        scratch.append(pltpu.VMEM((count * depth, features), jnp.bfloat16))
    return pl.pallas_call(
        functools.partial(ffn_kernel, count),
        out_shape=[jax.ShapeDtypeStruct((depth, features), jnp.bfloat16)] * count,
        in_specs=[vmem] * (count + 3),
        out_specs=[vmem] * count,
        scratch_shapes=scratch,
        compiler_params=pltpu.CompilerParams(vmem_limit_bytes=24 << 20),
        cost_estimate=pl.CostEstimate(
            flops=6 * count * depth * features * units,
            transcendentals=count * depth * units,
            bytes_accessed=6 * features * units + 4 * count * depth * features,
        ),
    )(*pieces, *weights)


def body(
    attn_out,
    residual,
    proj_weight,
    norm_gain,
    gate_weight,
    up_weight,
    down_weight,
    routes,
    route_weights,
):
    model_parts = lax.axis_size("mp")
    unit_parts = lax.axis_size("expert")
    row_count = residual.shape[0]
    features = residual.shape[1]
    blocks = attn_out.reshape(model_parts, unit_parts, row_count, attn_out.shape[1])
    picked = lax.dynamic_index_in_dim(blocks, lax.axis_index("expert"), axis=1, keepdims=False)
    picked = picked.reshape(model_parts * row_count, attn_out.shape[1])
    parts = jnp.dot(picked, proj_weight, preferred_element_type=jnp.float32).astype(jnp.float16)
    parts = parts.reshape(model_parts, row_count, features)
    parts = lax.all_to_all(parts, "mp", split_axis=0, concat_axis=0, tiled=True)
    hidden_state = residual + jnp.sum(parts, axis=0, dtype=jnp.float32)
    inverse_rms = lax.rsqrt(jnp.mean(hidden_state * hidden_state, axis=1, keepdims=True) + EPSILON)
    normed = (hidden_state * inverse_rms * norm_gain).astype(jnp.bfloat16)
    expert_ids = routes.reshape(-1)
    onehot = (expert_ids[:, None] == jnp.arange(EXPERTS, dtype=jnp.int32)[None, :]).astype(
        jnp.int32
    )
    before = jnp.cumsum(onehot, axis=0) - onehot
    position = jnp.sum(before * onehot, axis=1)
    target = (expert_ids * MOST + position).reshape(row_count, 2)
    slots = jnp.arange(EXPERTS * MOST, dtype=jnp.int32)
    first = target[:, 0][:, None] == slots[None, :]
    second = target[:, 1][:, None] == slots[None, :]
    placement = (first | second).astype(jnp.bfloat16)
    outgoing = lax.dot_general(
        placement, normed, (((0,), (0,)), ((), ())), preferred_element_type=jnp.float32
    ).astype(jnp.bfloat16)
    outgoing = outgoing.reshape(model_parts, MOST, features)
    arrived = lax.all_to_all(outgoing, "mp", split_axis=0, concat_axis=0, tiled=True)
    own = arrived.reshape(model_parts * MOST, features)

    weights = load(gate_weight[0], up_weight[0], down_weight[0])

    def shift(value, by):
        return lax.ppermute(
            value, "expert", [(i, (i + by) % unit_parts) for i in range(unit_parts)]
        )

    before_rows = shift(own, 1)
    after_rows = shift(own, -1)
    (own_sum,) = ffn([own], *weights)
    far_rows = shift(lax.optimization_barrier((own, own_sum))[0], 2)
    before_rows, after_rows = lax.optimization_barrier((before_rows, after_rows))
    (before_sum,) = ffn([before_rows], *weights)
    back_after = shift(before_sum, -1)
    after_rows = lax.optimization_barrier((after_rows, before_sum))[0]
    (after_sum,) = ffn([after_rows], *weights)
    back_before = shift(after_sum, 1)
    far_rows = lax.optimization_barrier((far_rows, after_sum))[0]
    (far_sum,) = ffn([far_rows], *weights)
    back_far = shift(far_sum, 2)
    near = own_sum.astype(jnp.float32) + back_after.astype(jnp.float32)
    near = lax.optimization_barrier(near) + back_before.astype(jnp.float32)
    outputs = lax.optimization_barrier(near) + back_far.astype(jnp.float32)
    outputs = outputs.astype(jnp.bfloat16).reshape(model_parts, MOST, features)
    outputs = lax.all_to_all(outputs, "mp", split_axis=0, concat_axis=0, tiled=True)
    expert_out = outputs.reshape(EXPERTS * MOST, features)
    one = jnp.dot(first.astype(jnp.bfloat16), expert_out, preferred_element_type=jnp.float32)
    two = jnp.dot(second.astype(jnp.bfloat16), expert_out, preferred_element_type=jnp.float32)
    return hidden_state + route_weights[:, 0:1] * one + route_weights[:, 1:2] * two


def solution(mesh):
    in_specs = (
        P("dp", "mp"),
        P(("dp", "mp", "expert"), None),
        P("mp", None),
        P(),
        P("mp", None, "expert"),
        P("mp", None, "expert"),
        P("mp", "expert", None),
        P(("dp", "mp", "expert"), None),
        P(("dp", "mp", "expert"), None),
    )
    out_specs = P(("dp", "mp", "expert"), None)
    return jax.shard_map(body, mesh=mesh, in_specs=in_specs, out_specs=out_specs, check_vma=False)
```

```python
import functools

import jax
import jax.numpy as jnp
from jax import lax
from jax.experimental import pallas as pl
from jax.experimental.pallas import tpu as pltpu
from jax.sharding import PartitionSpec as P

EXPERTS = 8
MOST = 16
EPSILON = 1e-06

UNIT_CHUNK = 512
OUT_CHUNK = 1152
ROW_BLOCK = 32


def pick_kernel(place_ref, columns_ref, out_ref):
    count = columns_ref.shape[1]
    rows = out_ref.shape[0]
    row = lax.broadcasted_iota(jnp.int32, (rows, count), 0)
    source = lax.broadcasted_iota(jnp.int32, (rows, count), 1)
    group = count // rows
    wanted = (row // ROW_BLOCK * group + place_ref[0]) * ROW_BLOCK + row % ROW_BLOCK
    pick = (source == wanted).astype(jnp.float32).astype(jnp.bfloat16)
    out_ref[...] = lax.dot_general(
        pick,
        columns_ref[...],
        (((1,), (1,)), ((), ())),
        preferred_element_type=jnp.float32,
    ).astype(jnp.bfloat16)


def pick_rows(place, attn_out, rows):
    vmem = pl.BlockSpec(memory_space=pltpu.VMEM)
    return pl.pallas_call(
        pick_kernel,
        out_shape=jax.ShapeDtypeStruct((rows, attn_out.shape[1]), attn_out.dtype),
        in_specs=[pl.BlockSpec(memory_space=pltpu.SMEM), vmem],
        out_specs=vmem,
        compiler_params=pltpu.CompilerParams(vmem_limit_bytes=16 << 20),
    )(place.reshape(1), attn_out.T)


def load_kernel(*refs):
    count = (len(refs) - 1) // 2
    sems = refs[-1]
    copies = [
        pltpu.make_async_copy(refs[i], refs[count + i], sems.at[i]) for i in range(count)
    ]
    for copy in copies:
        copy.start()
    for copy in copies:
        copy.wait()


def load(*weights):
    hbm = pl.BlockSpec(memory_space=pltpu.HBM)
    vmem = pl.BlockSpec(memory_space=pltpu.VMEM)
    total = sum(w.size * w.dtype.itemsize for w in weights)
    return pl.pallas_call(
        load_kernel,
        out_shape=[pltpu.VMEM(w.shape, w.dtype) for w in weights],
        in_specs=[hbm] * len(weights),
        out_specs=[vmem] * len(weights),
        scratch_shapes=[pltpu.SemaphoreType.DMA((len(weights),))],
        compiler_params=pltpu.CompilerParams(vmem_limit_bytes=20 << 20),
        cost_estimate=pl.CostEstimate(flops=0, transcendentals=0, bytes_accessed=2 * total),
    )(*(pltpu.with_memory_space_constraint(w, pltpu.HBM) for w in weights))


def ffn_kernel(count, *refs):
    row_refs, refs = refs[:count], refs[count:]
    (gate_ref, up_ref, down_ref), refs = refs[:3], refs[3:]
    out_refs, refs = refs[:count], refs[count:]
    act_ref = refs[0]
    depth = row_refs[0].shape[0]
    if count == 1:
        rows_ref = row_refs[0]
    else:
        rows_ref = refs[1]
        for piece in range(count):
            rows_ref[pl.ds(piece * depth, depth), :] = row_refs[piece][...]
    for start in range(0, act_ref.shape[1], UNIT_CHUNK):
        at = pl.ds(start, UNIT_CHUNK)
        gate = jnp.dot(rows_ref[...], gate_ref[:, at], preferred_element_type=jnp.float32)
        up = jnp.dot(rows_ref[...], up_ref[:, at], preferred_element_type=jnp.float32)
        act_ref[:, at] = (gate / (1.0 + jnp.exp(-gate)) * up).astype(jnp.bfloat16)
    for start in range(0, down_ref.shape[1], OUT_CHUNK):
        at = pl.ds(start, OUT_CHUNK)
        out = jnp.dot(act_ref[...], down_ref[:, at], preferred_element_type=jnp.float32)
        for piece in range(count):
            out_refs[piece][:, at] = out[piece * depth : (piece + 1) * depth].astype(jnp.bfloat16)


def ffn(pieces, *weights):
    count = len(pieces)
    depth, features = pieces[0].shape
    units = weights[0].shape[1]
    vmem = pl.BlockSpec(memory_space=pltpu.VMEM)
    scratch = [pltpu.VMEM((count * depth, units), jnp.bfloat16)]
    if count > 1:
        scratch.append(pltpu.VMEM((count * depth, features), jnp.bfloat16))
    return pl.pallas_call(
        functools.partial(ffn_kernel, count),
        out_shape=[jax.ShapeDtypeStruct((depth, features), jnp.bfloat16)] * count,
        in_specs=[vmem] * (count + 3),
        out_specs=[vmem] * count,
        scratch_shapes=scratch,
        compiler_params=pltpu.CompilerParams(vmem_limit_bytes=24 << 20),
        cost_estimate=pl.CostEstimate(
            flops=6 * count * depth * features * units,
            transcendentals=count * depth * units,
            bytes_accessed=6 * features * units + 4 * count * depth * features,
        ),
    )(*pieces, *weights)


def body(
    attn_out,
    residual,
    proj_weight,
    norm_gain,
    gate_weight,
    up_weight,
    down_weight,
    routes,
    route_weights,
):
    model_parts = lax.axis_size("mp")
    unit_parts = lax.axis_size("expert")
    row_count = residual.shape[0]
    features = residual.shape[1]
    picked = pick_rows(lax.axis_index("expert"), attn_out, model_parts * row_count)
    parts = jnp.dot(picked, proj_weight, preferred_element_type=jnp.float32).astype(jnp.float16)
    parts = parts.reshape(model_parts, row_count, features)
    parts = lax.all_to_all(parts, "mp", split_axis=0, concat_axis=0, tiled=True)
    hidden_state = residual + jnp.sum(parts, axis=0, dtype=jnp.float32)
    inverse_rms = lax.rsqrt(jnp.mean(hidden_state * hidden_state, axis=1, keepdims=True) + EPSILON)
    normed = (hidden_state * inverse_rms * norm_gain).astype(jnp.bfloat16)
    expert_ids = routes.reshape(-1)
    onehot = (expert_ids[:, None] == jnp.arange(EXPERTS, dtype=jnp.int32)[None, :]).astype(
        jnp.int32
    )
    before = jnp.cumsum(onehot, axis=0) - onehot
    position = jnp.sum(before * onehot, axis=1)
    target = (expert_ids * MOST + position).reshape(row_count, 2)
    slots = jnp.arange(EXPERTS * MOST, dtype=jnp.int32)
    first = target[:, 0][:, None] == slots[None, :]
    second = target[:, 1][:, None] == slots[None, :]
    placement = (first | second).astype(jnp.bfloat16)
    outgoing = lax.dot_general(
        placement, normed, (((0,), (0,)), ((), ())), preferred_element_type=jnp.float32
    ).astype(jnp.bfloat16)
    outgoing = outgoing.reshape(model_parts, MOST, features)
    arrived = lax.all_to_all(outgoing, "mp", split_axis=0, concat_axis=0, tiled=True)
    own = arrived.reshape(model_parts * MOST, features)

    weights = load(gate_weight[0], up_weight[0], down_weight[0])

    def shift(value, by):
        return lax.ppermute(
            value, "expert", [(i, (i + by) % unit_parts) for i in range(unit_parts)]
        )

    before_rows = shift(own, 1)
    after_rows = shift(own, -1)
    (own_sum,) = ffn([own], *weights)
    far_rows = shift(lax.optimization_barrier((own, own_sum))[0], 2)
    before_rows, after_rows = lax.optimization_barrier((before_rows, after_rows))
    (before_sum,) = ffn([before_rows], *weights)
    back_after = shift(before_sum, -1)
    after_rows = lax.optimization_barrier((after_rows, before_sum))[0]
    (after_sum,) = ffn([after_rows], *weights)
    back_before = shift(after_sum, 1)
    far_rows = lax.optimization_barrier((far_rows, after_sum))[0]
    (far_sum,) = ffn([far_rows], *weights)
    back_far = shift(far_sum, 2)
    near = own_sum.astype(jnp.float32) + back_after.astype(jnp.float32)
    near = lax.optimization_barrier(near) + back_before.astype(jnp.float32)
    outputs = lax.optimization_barrier(near) + back_far.astype(jnp.float32)
    outputs = outputs.astype(jnp.bfloat16).reshape(model_parts, MOST, features)
    outputs = lax.all_to_all(outputs, "mp", split_axis=0, concat_axis=0, tiled=True)
    expert_out = outputs.reshape(EXPERTS * MOST, features)
    one = jnp.dot(first.astype(jnp.bfloat16), expert_out, preferred_element_type=jnp.float32)
    two = jnp.dot(second.astype(jnp.bfloat16), expert_out, preferred_element_type=jnp.float32)
    return hidden_state + route_weights[:, 0:1] * one + route_weights[:, 1:2] * two


def solution(mesh):
    in_specs = (
        P("dp", "mp"),
        P(("dp", "mp", "expert"), None),
        P("mp", None),
        P(),
        P("mp", None, "expert"),
        P("mp", None, "expert"),
        P("mp", "expert", None),
        P(("dp", "mp", "expert"), None),
        P(("dp", "mp", "expert"), None),
    )
    out_specs = P(("dp", "mp", "expert"), None)
    return jax.shard_map(body, mesh=mesh, in_specs=in_specs, out_specs=out_specs, check_vma=False)
```
